32 devices in a mesh: dp: 16 (over z, y, core), space: 2 (over x).
Axes of the slice: x: 2, y: 2, z: 4, core: 2. Of those that a mesh axis runs over, the one named last changes fastest.
Arguments:
- volumes: bfloat16 [16, 32, 8, 8, 128], P('dp', None, 'space'), may hold values from -6 to 6
- w_first: bfloat16 [864, 64], P('dp'), may hold values from -0.21875 to 0.21875
- w_second: bfloat16 [1728, 128], P('dp'), may hold values from -0.4375 to 0.4375
- cotangent: bfloat16 [16, 128, 2, 2, 32], P('dp', None, 'space'), may hold values from -96 to 96
Outputs:
- pooled: bfloat16 [16, 128, 2, 2, 32], P('dp', None, 'space')
- volume_grad: bfloat16 [16, 32, 8, 8, 128], P('dp', None, 'space')
- grad_first: float32 [864, 64], P('dp')
- grad_second: float32 [1728, 128], P('dp')
The draws below stay inside these ranges and needn't reach their ends.
All inputs are finite; a program needn't handle non-finite values.
Results may differ from the reference program's by a relative error of at most 0.023.
Values may be sent and summed in bfloat16 or wider, within the bound.
No kernel may reach another device: no remote copies, remote signals or barrier semaphores. Data moves between devices by JAX's collectives and lax.ppermute only.
A program may use at most 128 MiB of HBM per device.

```python
import jax
import jax.numpy as jnp
from jax import lax

C0 = 32
C1 = 64
C2 = 128
Y = 8
Z = 128
SAMPLES = 16
X = 8
K1 = 864
K2 = 1728


def level_of(rng, extent, cuts, low, top_value):
    loudness, own = 1.0, jax.random.fold_in(rng, 6)
    for dim, blocks in cuts:
        draws = jnp.exp(jax.random.uniform(jax.random.fold_in(own, dim), (blocks,), jnp.float32, low / len(cuts), top_value / len(cuts)))
        loudness = loudness * jnp.repeat(draws, extent[dim] // blocks).reshape([-1 if axis == dim else 1 for axis in range(len(extent))])
    return loudness


def gaussian(stream_key, dims, deviation, limit, cuts=(), kind=jnp.bfloat16):
    gain = level_of(stream_key, dims, cuts, -0.22, 0.18) if cuts else 1.0
    entries = jax.random.normal(stream_key, dims, jnp.float32) * deviation * gain
    return jnp.minimum(jnp.maximum(entries, -limit), limit).astype(kind)


def setup_inputs(seed: int = 0) -> dict:
    streams_of = jax.random.split(jax.random.key(seed), 5)
    volumes = gaussian(streams_of[0], (SAMPLES, C0, X, Y, Z), 1.0, 6.0, ((0, 16), (2, 2)))
    w_first = gaussian(streams_of[1], (K1, C1), K1 ** -0.5, 0.21875, ((0, 16),))
    w_second = gaussian(streams_of[2], (K2, C2), (K2 // 8) ** -0.5, 0.4375, ((0, 16),))
    cotangent = gaussian(streams_of[3], (SAMPLES, C2, X // 4, Y // 4, Z // 4), 16.0, 96.0, ((0, 16), (2, 2)))
    return {"volumes": volumes, "w_first": w_first, "w_second": w_second, "cotangent": cotangent}


def conv_forward(field, weight):
    in_width, extent_x, extent_y, extent_z = field.shape
    out_width = weight.shape[1]
    padded = jnp.pad(field.astype(jnp.float32), ((0, 0), (1, 1), (1, 1), (1, 1)))
    kernel = weight.astype(jnp.float32).reshape(3, 3, 3, in_width, out_width)
    summed = jnp.zeros((out_width, extent_x, extent_y, extent_z), jnp.float32)
    for along_x in range(3):
        for along_y in range(3):
            for along_z in range(3):
                window = padded[:, along_x:along_x + extent_x, along_y:along_y + extent_y, along_z:along_z + extent_z]
                summed = summed + jnp.einsum('ixyz,io->oxyz', window, kernel[along_x, along_y, along_z])
    return summed

def conv_input_grad(grads, weight, in_width):
    out_width, extent_x, extent_y, extent_z = grads.shape
    padded = jnp.pad(grads.astype(jnp.float32), ((0, 0), (1, 1), (1, 1), (1, 1)))
    kernel = weight.astype(jnp.float32).reshape(3, 3, 3, in_width, out_width)
    summed = jnp.zeros((in_width, extent_x, extent_y, extent_z), jnp.float32)
    for along_x in range(3):
        for along_y in range(3):
            for along_z in range(3):
                window = padded[:, 2 - along_x:2 - along_x + extent_x, 2 - along_y:2 - along_y + extent_y, 2 - along_z:2 - along_z + extent_z]
                summed = summed + jnp.einsum('oxyz,io->ixyz', window, kernel[along_x, along_y, along_z])
    return summed

def conv_weight_grad(field, grads):
    in_width, extent_x, extent_y, extent_z = field.shape
    padded = jnp.pad(field.astype(jnp.float32), ((0, 0), (1, 1), (1, 1), (1, 1)))
    grads_wide = grads.astype(jnp.float32)
    pieces = []
    for along_x in range(3):
        for along_y in range(3):
            for along_z in range(3):
                window = padded[:, along_x:along_x + extent_x, along_y:along_y + extent_y, along_z:along_z + extent_z]
                pieces.append(jnp.einsum('ixyz,oxyz->io', window, grads_wide))
    return jnp.stack(pieces).reshape(27 * in_width, grads.shape[0])

def pooling(field):
    width, extent_x, extent_y, extent_z = field.shape
    blocks = field.reshape(width, extent_x // 2, 2, extent_y // 2, 2, extent_z // 2, 2)
    return lax.optimization_barrier(jnp.mean(blocks, axis=(2, 4, 6)))

def spread_up(field):
    width, extent_x, extent_y, extent_z = field.shape
    blocks = jnp.broadcast_to(field[:, :, None, :, None, :, None], (width, extent_x, 2, extent_y, 2, extent_z, 2))
    return blocks.reshape(width, 2 * extent_x, 2 * extent_y, 2 * extent_z)

def silu_slope(values):
    sigma = jax.nn.sigmoid(values)
    return sigma * (1.0 + values * (1.0 - sigma))

def reference(volumes, w_first, w_second, cotangent):
    in_width = volumes.shape[1]
    mid_width = w_first.shape[1]

    def per_sample(running, sample_pair):
        volume, cotangent_one = sample_pair
        first_pre = conv_forward(volume, w_first)
        first_pool = pooling(jax.nn.silu(first_pre)).astype(jnp.bfloat16)
        second_pre = conv_forward(first_pool, w_second)
        pooled_one = pooling(jax.nn.silu(second_pre)).astype(jnp.bfloat16)
        second_delta = (spread_up(cotangent_one.astype(jnp.float32)) * 0.125 * silu_slope(second_pre)).astype(jnp.bfloat16)
        grad_two = conv_weight_grad(first_pool, second_delta)
        pool_grad = conv_input_grad(second_delta, w_second, mid_width).astype(jnp.bfloat16)
        first_delta = (spread_up(pool_grad.astype(jnp.float32)) * 0.125 * silu_slope(first_pre)).astype(jnp.bfloat16)
        grad_one = conv_weight_grad(volume, first_delta)
        input_grad = conv_input_grad(first_delta, w_first, in_width).astype(jnp.bfloat16)
        return ((running[0] + grad_one, running[1] + grad_two), (pooled_one, input_grad))
    start = (jnp.zeros(w_first.shape, jnp.float32), jnp.zeros(w_second.shape, jnp.float32))
    sums, stacked = lax.scan(per_sample, start, (volumes, cotangent))
    factor_one = float(SAMPLES * X * Y * Z) ** (-0.5)
    factor_two = float(SAMPLES * X * Y * Z // 8) ** (-0.5)
    return (stacked[0], stacked[1], sums[0] * factor_one, sums[1] * factor_two)
```

```python
import functools

import jax
import jax.numpy as jnp
from jax import lax
from jax.experimental import pallas as pl
from jax.experimental.pallas import tpu as pltpu
from jax.sharding import PartitionSpec as P

BF = jnp.bfloat16
F32 = jnp.float32


def dot(a, b):
    return jnp.dot(a, b, preferred_element_type=F32)


def dot_nt(a, b):
    return lax.dot_general(a, b, (((1,), (1,)), ((), ())), preferred_element_type=F32)


def iota(shape, dim):
    return lax.broadcasted_iota(jnp.int32, shape, dim)


def eye(n):
    return (iota((n, n), 0) == iota((n, n), 1)).astype(F32).astype(BF)


def roll_z(x, by):
    lane = iota(x.shape, 1)
    edge = 0 if by == 1 else 127
    return jnp.where(lane == edge, 0.0, pltpu.roll(x, by % 128, 1))


def roll_yz(x, db, dc):
    if db == 0 and dc == 0:
        return x
    lane = iota(x.shape, 1)
    y, z = lane // 64 + db, lane % 64 + dc
    inside = (y >= 0) & (y < 4) & (z >= 0) & (z < 64)
    return jnp.where(inside, pltpu.roll(x, (-(db * 64 + dc)) % 256, 1), 0.0)


def unpack_weights(me, g0_ref, g1_ref, w1f, w2f):
    for d in range(16):
        k = jnp.bitwise_xor(me, d)
        core, rest = k % 2, (k // 2) % 2 * 4 + k // 4
        blk = lax.select(core == 0, g0_ref[rest], g1_ref[rest])
        blk = blk.astype(F32)
        w2f[108 * d : 108 * d + 108, :] = blk[0:108]
        w1f[54 * d : 54 * d + 27, :] = blk[108:135, 0:64]
        w1f[54 * d + 27 : 54 * d + 54, :] = blk[108:135, 64:128]


def fused_kernel(
    factor_one, factor_two,
    pos, vo, vx, co, cx, ga, gb,
    pooled_out, keep_out, send_out, dp_out, w1_out,
    w1f, w2f, w2s, vs, slope, fpl, fs, d2p, t2, wcat, acc1, g2f, g1f, pg, chunk,
):
    me, s = pos[0], pos[1]
    unpack_weights(me, ga, gb, w1f, w2f)
    w1_out[...] = w1f[...].astype(BF)
    w2s[...] = w2f[...].astype(BF)
    vs[...] = jnp.zeros(vs.shape, BF)
    for p in range(4):
        vs[4 * s + 1 + p, :, 128:1152] = vo[p]
        vs[4 * (1 - s) + 1 + p, :, 128:1152] = vx[p]
    id64, id128 = eye(64), eye(128)
    lhs1 = jnp.concatenate(
        [
            dot_nt(
                id64,
                jnp.concatenate(
                    [w1f[(ab * 3 + c) * 32 : (ab * 3 + c) * 32 + 32, :] for ab in range(9)], axis=0
                ).astype(BF),
            ).astype(BF)
            for c in range(3)
        ],
        axis=0,
    )
    pool_m = (iota((256, 128), 0) // 2 == iota((256, 128), 1)).astype(F32).astype(BF)

    def cols_of(x):
        return jnp.concatenate(
            [vs[x + a, :, b * 128 : b * 128 + 1024] for a in range(3) for b in range(3)], axis=0
        )

    def first(x2, carry):
        total = [jnp.zeros((64, 128), F32) for _ in range(4)]
        for dx in range(2):
            x = 2 * x2 + dx
            prod = dot(lhs1, cols_of(x))
            for y in range(8):
                part = prod[:, y * 128 : y * 128 + 128]
                pre = part[64:128] + roll_z(part[0:64], 1) + roll_z(part[128:192], -1)
                sig = jax.nn.sigmoid(pre)
                act = pre * sig
                slope[x, :, y * 128 : y * 128 + 128] = sig + act * (1.0 - sig)
                total[y // 2] = total[y // 2] + act
        for h in range(2):
            pair = jnp.concatenate([total[2 * h], total[2 * h + 1]], axis=1)
            hi = pair.astype(BF)
            lo = (pair - hi.astype(F32)).astype(BF)
            fpl[x2, :, h * 128 : h * 128 + 128] = (
                (dot(hi, pool_m) + dot(lo, pool_m)) * 0.125
            ).astype(BF).astype(F32)
        return carry

    lax.fori_loop(0, 4, first, 0)

    fs[0] = jnp.zeros((576, 256), BF)
    fs[5] = jnp.zeros((576, 256), BF)
    d2p[0] = jnp.zeros((128, 256), BF)
    d2p[5] = jnp.zeros((128, 256), BF)

    def shifts(x2, carry):
        plane = fpl[x2]
        for bc in range(9):
            fs[x2 + 1, bc * 64 : bc * 64 + 64, :] = roll_yz(plane, bc // 3 - 1, bc % 3 - 1).astype(BF)
        return carry

    lax.fori_loop(0, 4, shifts, 0)
    w2t = dot_nt(id128, w2s[...]).astype(BF)
    col = iota((64, 256), 1)
    spread2 = (iota((64, 256), 0) == (col // 128) * 32 + (col % 64) // 2).astype(F32).astype(BF)
    row = iota((256, 64), 0)
    pool2 = (iota((256, 64), 1) == (row // 128) * 32 + (row % 64) // 2).astype(F32).astype(BF)

    def second(x4, carry):
        cot = lax.select(x4 == s, co[...], cx[...])
        wide = dot(cot, spread2) * 0.125
        total = jnp.zeros((128, 256), F32)
        for dx in range(2):
            x2 = 2 * x4 + dx
            rhs = jnp.concatenate([fs[x2], fs[x2 + 1], fs[x2 + 2]], axis=0)
            pre = dot(w2t, rhs)
            sig = jax.nn.sigmoid(pre)
            act = pre * sig
            total = total + act
            d2p[x2 + 1] = (wide * (sig + act * (1.0 - sig))).astype(BF)
        t2[x4] = total
        return carry

    lax.fori_loop(0, 2, second, 0)
    mine = t2[s]
    hi = mine.astype(BF)
    lo = (mine - hi.astype(F32)).astype(BF)
    pooled_out[...] = ((dot(hi, pool2) + dot(lo, pool2)) * 0.125).astype(BF)

    deltas = jnp.concatenate([d2p[1], d2p[2], d2p[3], d2p[4]], axis=1)
    for a in range(3):
        lhs = jnp.concatenate([fs[a], fs[a + 1], fs[a + 2], fs[a + 3]], axis=1)
        g2f[a * 576 : a * 576 + 576, :] = dot_nt(lhs, deltas) * factor_two
        wcat[:, a * 128 : a * 128 + 128] = w2s[a * 576 : a * 576 + 576, :]

    spread1 = (iota((128, 256), 0) == iota((128, 256), 1) // 2).astype(F32).astype(BF)
    acc1[...] = jnp.zeros(acc1.shape, F32)
    dp_out[...] = jnp.zeros(dp_out.shape, BF)

    def back(x2, carry):
        rhs = jnp.concatenate([d2p[x2 + 2], d2p[x2 + 1], d2p[x2]], axis=0)
        prod = dot(wcat[...], rhs)
        grad = jnp.zeros((64, 256), F32)
        for bc in range(9):
            grad = grad + roll_yz(prod[bc * 64 : bc * 64 + 64], 1 - bc // 3, 1 - bc % 3)
        grad = grad.astype(BF)
        for h in range(2):
            wide = dot(grad[:, h * 128 : h * 128 + 128], spread1) * 0.125
            for dx in range(2):
                for y in range(4):
                    lanes = slice((4 * h + y) * 128, (4 * h + y) * 128 + 128)
                    value = wide[:, (y // 2) * 128 : (y // 2) * 128 + 128] * slope[2 * x2 + dx, :, lanes]
                    pg[dx, 64:128, lanes] = value.astype(BF)
                    pg[dx, 0:64, lanes] = roll_z(value, -1).astype(BF)
                    pg[dx, 128:192, lanes] = roll_z(value, 1).astype(BF)
        for dx in range(2):
            x = 2 * x2 + dx
            dp_out[x + 1, :, 128:1152] = pg[dx, 64:128, :]
            acc1[...] += dot_nt(cols_of(x), pg[dx])
        return carry

    lax.fori_loop(0, 4, back, 0)
    for ab in range(9):
        for c in range(3):
            g1f[(ab * 3 + c) * 32 : (ab * 3 + c) * 32 + 32, :] = (
                acc1[ab * 32 : ab * 32 + 32, c * 64 : c * 64 + 64] * factor_one
            )
    chunk[...] = jnp.zeros(chunk.shape, F32)
    for d in range(16):
        chunk[0:108, :] = g2f[108 * d : 108 * d + 108, :]
        chunk[108:135, 0:64] = g1f[54 * d : 54 * d + 27, :]
        chunk[108:135, 64:128] = g1f[54 * d + 27 : 54 * d + 54, :]
        k = jnp.bitwise_xor(me, d)
        place = (k // 2) % 2 * 4 + k // 4

        @pl.when(k % 2 == 0)
        def _():
            keep_out[place] = chunk[...].astype(BF)

        @pl.when(k % 2 == 1)
        def _():
            send_out[place] = chunk[...].astype(BF)


def volume_kernel(pos, dp, w1, out, wd):
    s = pos[1]
    for ab in range(9):
        wd[:, ab * 64 : ab * 64 + 64] = w1[ab * 96 : ab * 96 + 96, :]
    lhs = wd[...]

    def plane(p, carry):
        x = 4 * s + p
        rhs = jnp.concatenate(
            [
                dp[x + 2 - a, :, (2 - b) * 128 : (2 - b) * 128 + 1024]
                for a in range(3)
                for b in range(3)
            ],
            axis=0,
        )
        prod = dot(lhs, rhs)
        for y in range(8):
            part = prod[:, y * 128 : y * 128 + 128]
            out[p, :, y * 128 : y * 128 + 128] = (
                part[32:64] + roll_z(part[0:32], -1) + roll_z(part[64:96], 1)
            ).astype(BF)
        return carry

    lax.fori_loop(0, 4, plane, 0)


def fused_call(factor_one, factor_two, pos, vo, vx, co, cx, ga, gb):
    vmem = pl.BlockSpec(memory_space=pltpu.VMEM)
    return pl.pallas_call(
        functools.partial(fused_kernel, factor_one, factor_two),
        out_shape=(
            jax.ShapeDtypeStruct((128, 64), BF),
            jax.ShapeDtypeStruct((8, 136, 128), BF),
            jax.ShapeDtypeStruct((8, 136, 128), BF),
            jax.ShapeDtypeStruct((10, 64, 1280), BF),
            jax.ShapeDtypeStruct((864, 64), BF),
        ),
        in_specs=[pl.BlockSpec(memory_space=pltpu.SMEM)] + [vmem] * 6,
        out_specs=(vmem,) * 5,
        scratch_shapes=[
            pltpu.VMEM((864, 64), F32),
            pltpu.VMEM((1728, 128), F32),
            pltpu.VMEM((1728, 128), BF),
            pltpu.VMEM((10, 32, 1280), BF),
            pltpu.VMEM((8, 64, 1024), F32),
            pltpu.VMEM((4, 64, 256), F32),
            pltpu.VMEM((6, 576, 256), BF),
            pltpu.VMEM((6, 128, 256), BF),
            pltpu.VMEM((2, 128, 256), F32),
            pltpu.VMEM((576, 384), BF),
            pltpu.VMEM((288, 192), F32),
            pltpu.VMEM((1728, 128), F32),
            pltpu.VMEM((864, 64), F32),
            pltpu.VMEM((2, 192, 1024), BF),
            pltpu.VMEM((136, 128), F32),
        ],
        compiler_params=pltpu.CompilerParams(vmem_limit_bytes=48 << 20),
        cost_estimate=pl.CostEstimate(flops=4_000_000_000, bytes_accessed=6_000_000, transcendentals=700_000),
        name="fused",
    )(pos, vo, vx, co, cx, ga, gb)


def volume_call(pos, dp, w1):
    vmem = pl.BlockSpec(memory_space=pltpu.VMEM)
    return pl.pallas_call(
        volume_kernel,
        out_shape=jax.ShapeDtypeStruct((4, 32, 1024), BF),
        in_specs=[pl.BlockSpec(memory_space=pltpu.SMEM), vmem, vmem],
        out_specs=vmem,
        scratch_shapes=[pltpu.VMEM((96, 576), BF)],
        compiler_params=pltpu.CompilerParams(vmem_limit_bytes=16 << 20),
        cost_estimate=pl.CostEstimate(flops=1_000_000_000, bytes_accessed=3_000_000, transcendentals=0),
        name="volume",
    )(pos, dp, w1)


def fits(volumes, w_first, w_second, cotangent):
    return (
        lax.axis_size("dp") == 16
        and lax.axis_size("space") == 2
        and volumes.shape == (1, 32, 4, 8, 128)
        and w_first.shape == (54, 64)
        and w_second.shape == (108, 128)
        and cotangent.shape == (1, 128, 1, 2, 32)
    )


def swap(x, bit):
    return lax.ppermute(x, "dp", [(i, i ^ bit) for i in range(16)])


def paired(volumes, w_first, w_second, cotangent):
    count = 16 * 2 * (volumes.size // 32)
    factor_one, factor_two = float(count) ** (-0.5), float(count // 8) ** (-0.5)
    pos = jnp.stack([lax.axis_index("dp"), lax.axis_index("space")]).astype(jnp.int32)
    own = jnp.transpose(volumes[0], (1, 0, 2, 3)).reshape(4, 32, 1024)
    cot = cotangent.reshape(128, 64)
    other = lax.ppermute(own, "space", [(0, 1), (1, 0)])
    cot_other = lax.ppermute(cot, "space", [(0, 1), (1, 0)])
    shard = jnp.concatenate(
        [
            w_second,
            jnp.concatenate([w_first[:27], w_first[27:]], axis=1),
            jnp.zeros((1, 128), BF),
        ],
        axis=0,
    )
    along_z = jnp.stack([shard] + [swap(shard, 4 * k) for k in range(1, 4)])
    along_y = jnp.concatenate([along_z, swap(along_z, 2)])
    across = swap(along_y, 1)
    pooled, keep, send, delta, w_one = fused_call(
        factor_one, factor_two, pos, own, other, cot, cot_other, along_y, across
    )
    part = (keep.astype(F32) + swap(send, 1).astype(F32)).astype(BF)
    part = (part[:4].astype(F32) + swap(part[4:], 2).astype(F32)).astype(BF)
    total = part[0].astype(F32)
    for k in range(1, 4):
        total = total + swap(part[k], 4 * k).astype(F32)
    grad = volume_call(pos, delta, w_one)
    grad = jnp.transpose(grad.reshape(4, 32, 8, 128), (1, 0, 2, 3))[None]
    share_one = jnp.concatenate([total[108:135, :64], total[108:135, 64:]], axis=0)
    return pooled.reshape(1, 128, 1, 2, 32), grad, share_one, total[:108]


def with_halo(block, sides, width):
    for axis, dim in sides:
        count = lax.axis_size(axis)
        forward = [(i, i + 1) for i in range(count - 1)]
        backward = [(target, source) for source, target in forward]
        low = lax.ppermute(
            lax.slice_in_dim(block, block.shape[dim] - width, None, axis=dim), axis, forward
        )
        high = lax.ppermute(lax.slice_in_dim(block, 0, width, axis=dim), axis, backward)
        block = jnp.concatenate([low, block, high], axis=dim)
    return block


def pad_sides(field):
    return jnp.pad(field, ((0, 0), (0, 0), (0, 0), (1, 1), (1, 1)))


def conv_forward(padded, weight):
    samples_here, in_width, depth_padded, extent_y, extent_z = padded.shape
    extent_x = depth_padded - 2
    out_width = weight.shape[1]
    framed = pad_sides(padded)
    kernel = weight.reshape(3, 3, 3, in_width, out_width)
    summed = jnp.zeros((samples_here, out_width, extent_x, extent_y, extent_z), jnp.float32)
    for along_x in range(3):
        for along_y in range(3):
            for along_z in range(3):
                window = framed[
                    :,
                    :,
                    along_x : along_x + extent_x,
                    along_y : along_y + extent_y,
                    along_z : along_z + extent_z,
                ]
                summed = summed + jnp.einsum(
                    "sixyz,io->soxyz",
                    window,
                    kernel[along_x, along_y, along_z],
                    preferred_element_type=jnp.float32,
                )
    return summed


def conv_input_grad(padded, weight, in_width):
    samples_here, out_width, depth_padded, extent_y, extent_z = padded.shape
    extent_x = depth_padded - 2
    framed = pad_sides(padded)
    kernel = weight.reshape(3, 3, 3, in_width, out_width)
    summed = jnp.zeros((samples_here, in_width, extent_x, extent_y, extent_z), jnp.float32)
    for along_x in range(3):
        for along_y in range(3):
            for along_z in range(3):
                window = framed[
                    :,
                    :,
                    2 - along_x : 2 - along_x + extent_x,
                    2 - along_y : 2 - along_y + extent_y,
                    2 - along_z : 2 - along_z + extent_z,
                ]
                summed = summed + jnp.einsum(
                    "soxyz,io->sixyz",
                    window,
                    kernel[along_x, along_y, along_z],
                    preferred_element_type=jnp.float32,
                )
    return summed


def conv_weight_grad(padded, grads):
    samples_here, in_width, depth_padded, extent_y, extent_z = padded.shape
    extent_x = depth_padded - 2
    framed = pad_sides(padded)
    pieces = []
    for along_x in range(3):
        for along_y in range(3):
            for along_z in range(3):
                window = framed[
                    :,
                    :,
                    along_x : along_x + extent_x,
                    along_y : along_y + extent_y,
                    along_z : along_z + extent_z,
                ]
                pieces.append(
                    jnp.einsum("sixyz,soxyz->io", window, grads, preferred_element_type=jnp.float32)
                )
    return jnp.stack(pieces).reshape(27 * in_width, grads.shape[1])


def pooling(field):
    samples_here, width, extent_x, extent_y, extent_z = field.shape
    blocks = field.reshape(
        samples_here, width, extent_x // 2, 2, extent_y // 2, 2, extent_z // 2, 2
    )
    return jnp.mean(blocks, axis=(3, 5, 7))


def spread_up(field):
    samples_here, width, extent_x, extent_y, extent_z = field.shape
    blocks = jnp.broadcast_to(
        field[:, :, :, None, :, None, :, None],
        (samples_here, width, extent_x, 2, extent_y, 2, extent_z, 2),
    )
    return blocks.reshape(samples_here, width, 2 * extent_x, 2 * extent_y, 2 * extent_z)


def silu_slope(values):
    sigma = jax.nn.sigmoid(values)
    return sigma * (1.0 + values * (1.0 - sigma))


def general(volumes, w_first, w_second, cotangent):
    kernel_one, kernel_two = (
        lax.all_gather(w_first, "dp", axis=0, tiled=True),
        lax.all_gather(w_second, "dp", axis=0, tiled=True),
    )
    in_width = volumes.shape[1]
    mid_width = kernel_one.shape[1]
    count_one = lax.axis_size("dp") * lax.axis_size("space") * (volumes.size // in_width)
    factor_one = float(count_one) ** (-0.5)
    factor_two = float(count_one // 8) ** (-0.5)
    input_padded = with_halo(volumes, (("space", 2),), 1)
    first_pre = conv_forward(input_padded, kernel_one)
    first_pool = pooling(jax.nn.silu(first_pre)).astype(jnp.bfloat16)
    pool_padded = with_halo(first_pool, (("space", 2),), 1)
    second_pre = conv_forward(pool_padded, kernel_two)
    pooled = pooling(jax.nn.silu(second_pre)).astype(jnp.bfloat16)
    second_delta = (
        spread_up(cotangent.astype(jnp.float32)) * 0.125 * silu_slope(second_pre)
    ).astype(jnp.bfloat16)
    grad_two = conv_weight_grad(pool_padded, second_delta) * factor_two
    delta_padded = with_halo(second_delta, (("space", 2),), 1)
    pool_grad = conv_input_grad(delta_padded, kernel_two, mid_width).astype(jnp.bfloat16)
    first_delta = (spread_up(pool_grad.astype(jnp.float32)) * 0.125 * silu_slope(first_pre)).astype(
        jnp.bfloat16
    )
    grad_one = conv_weight_grad(input_padded, first_delta) * factor_one
    first_padded = with_halo(first_delta, (("space", 2),), 1)
    volume_grad = conv_input_grad(first_padded, kernel_one, in_width).astype(jnp.bfloat16)
    rows_one, rows_two = (
        lax.psum_scatter(
            grad_one.astype(jnp.bfloat16), "dp", scatter_dimension=0, tiled=True
        ).astype(jnp.float32),
        lax.psum_scatter(
            grad_two.astype(jnp.bfloat16), "dp", scatter_dimension=0, tiled=True
        ).astype(jnp.float32),
    )
    share_one, share_two = (
        lax.psum(rows_one.astype(jnp.bfloat16), "space").astype(jnp.float32),
        lax.psum(rows_two.astype(jnp.bfloat16), "space").astype(jnp.float32),
    )
    return (pooled, volume_grad, share_one, share_two)


def local(volumes, w_first, w_second, cotangent):
    if fits(volumes, w_first, w_second, cotangent):
        return paired(volumes, w_first, w_second, cotangent)
    return general(volumes, w_first, w_second, cotangent)


def solution(mesh):
    return jax.shard_map(
        local,
        mesh=mesh,
        in_specs=(
            P("dp", None, "space", None, None),
            P("dp", None),
            P("dp", None),
            P("dp", None, "space", None, None),
        ),
        out_specs=(
            P("dp", None, "space", None, None),
            P("dp", None, "space", None, None),
            P("dp", None),
            P("dp", None),
        ),
        check_vma=False,
    )
```

```python
import functools

import jax
import jax.numpy as jnp
from jax import lax
from jax.experimental import pallas as pl
from jax.experimental.pallas import tpu as pltpu
from jax.sharding import PartitionSpec as P


BF = jnp.bfloat16
F32 = jnp.float32
VMEM = pl.BlockSpec(memory_space=pltpu.VMEM)
SMEM = pl.BlockSpec(memory_space=pltpu.SMEM)


def dot(a, b):
    return jnp.dot(a, b, preferred_element_type=F32)


def dot_nt(a, b):
    return lax.dot_general(a, b, (((1,), (1,)), ((), ())), preferred_element_type=F32)


def iota(shape, dim):
    return lax.broadcasted_iota(jnp.int32, shape, dim)


def where_one(mask):
    return mask.astype(F32).astype(BF)


def eye(n):
    return where_one(iota((n, n), 0) == iota((n, n), 1))


def halves(x):
    hi = x.astype(BF)
    return hi, (x - hi.astype(F32)).astype(BF)


def roll_z(x, by):
    lane = iota(x.shape, 1)
    edge = 0 if by == 1 else 127
    return jnp.where(lane == edge, 0.0, pltpu.roll(x, by % 128, 1))


def roll_yz(x, db, dc):
    if db == 0 and dc == 0:
        return x
    lane = iota(x.shape, 1)
    y, z = lane // 64 + db, lane % 64 + dc
    inside = (y >= 0) & (y < 4) & (z >= 0) & (z < 64)
    return jnp.where(inside, pltpu.roll(x, (-(db * 64 + dc)) % 256, 1), 0.0)


def pack_kernel(first, second, out, wide, narrow):
    wide[...] = jnp.zeros(wide.shape, F32)
    wide[0:108, :] = second[...].astype(F32)
    narrow[...] = first[...].astype(F32)
    wide[112:139, 0:64] = narrow[0:27, :]
    wide[112:139, 64:128] = narrow[27:54, :]
    out[...] = wide[...].astype(BF)


def pack_call(first, second):
    return pl.pallas_call(
        pack_kernel,
        out_shape=jax.ShapeDtypeStruct((144, 128), BF),
        in_specs=[VMEM] * 2,
        out_specs=VMEM,
        scratch_shapes=[pltpu.VMEM((144, 128), F32), pltpu.VMEM((54, 64), F32)],
        compiler_params=pltpu.CompilerParams(vmem_limit_bytes=2 << 20),
        cost_estimate=pl.CostEstimate(flops=40_000, bytes_accessed=80_000, transcendentals=0),
        name="pack",
    )(first, second)


def finish_kernel(kept, one, two, three, first, second, total):
    total[...] = (
        kept[0].astype(F32) + one[...].astype(F32) + two[...].astype(F32) + three[...].astype(F32)
    )
    second[...] = total[0:108, :]
    first[0:27, :] = total[112:139, 0:64]
    first[27:54, :] = total[112:139, 64:128]


def finish_call(kept, pieces):
    return pl.pallas_call(
        finish_kernel,
        out_shape=(
            jax.ShapeDtypeStruct((54, 64), F32),
            jax.ShapeDtypeStruct((108, 128), F32),
        ),
        in_specs=[VMEM] * 4,
        out_specs=(VMEM,) * 2,
        scratch_shapes=[pltpu.VMEM((144, 128), F32)],
        compiler_params=pltpu.CompilerParams(vmem_limit_bytes=2 << 20),
        cost_estimate=pl.CostEstimate(flops=80_000, bytes_accessed=300_000, transcendentals=0),
        name="finish",
    )(kept, *pieces)


def shift_kernel(pos, own, other, out):
    s = pos[1]
    out[0] = jnp.zeros((96, 1024), BF)
    out[9] = jnp.zeros((96, 1024), BF)
    for p in range(4):
        for block, place in ((own, 4 * s + 1 + p), (other, 4 * (1 - s) + 1 + p)):
            out[place, 32:64, :] = block[p]
            for y in range(8):
                lanes = slice(y * 128, y * 128 + 128)
                line = block[p, :, lanes].astype(F32)
                out[place, 0:32, lanes] = roll_z(line, 1).astype(BF)
                out[place, 64:96, lanes] = roll_z(line, -1).astype(BF)


def shift_call(pos, own, other):
    return pl.pallas_call(
        shift_kernel,
        out_shape=jax.ShapeDtypeStruct((10, 96, 1024), BF),
        in_specs=[SMEM, VMEM, VMEM],
        out_specs=VMEM,
        compiler_params=pltpu.CompilerParams(vmem_limit_bytes=8 << 20),
        cost_estimate=pl.CostEstimate(flops=600_000, bytes_accessed=2_500_000, transcendentals=0),
        name="shift",
    )(pos, own, other)


def unpack_weights(me, near, far, w1f, w2f):
    for parity in range(2):

        @pl.when(me % 2 == parity)
        def _():
            for d in range(16):
                k = jnp.bitwise_xor(me, d)
                ref = near if d % 2 == parity else far
                blk = ref[(k // 2) % 2 * 4 + k // 4].astype(F32)
                w2f[108 * d : 108 * d + 108, :] = blk[0:108]
                w1f[54 * d : 54 * d + 27, :] = blk[112:139, 0:64]
                w1f[54 * d + 27 : 54 * d + 54, :] = blk[112:139, 64:128]


def fused_kernel(
    factor_one, factor_two,
    pos, v3, co, cx, near, far,
    pooled_out, keep_out, send_out, dp, w1_out,
    w1f, w2f, w2s, slope, fpl, fs, d2p, t2, g2f, g1w,
):
    me, s = pos[0], pos[1]
    unpack_weights(me, near, far, w1f, w2f)
    w1_out[...] = w1f[...].astype(BF)
    w2s[...] = w2f[...].astype(BF)
    id64, id128 = eye(64), eye(128)
    lhs1 = jnp.concatenate(
        [
            dot_nt(
                id64,
                jnp.concatenate(
                    [w1f[(a * 3 + b) * 96 : (a * 3 + b) * 96 + 96, :] for a in range(3)], axis=0
                ).astype(BF),
            ).astype(BF)
            for b in range(3)
        ],
        axis=0,
    )
    pool1 = where_one(iota((256, 128), 0) // 2 == iota((256, 128), 1))

    def cols_of(x):
        return jnp.concatenate([v3[x], v3[x + 1], v3[x + 2]], axis=0)

    for x2 in range(4):
        total = [jnp.zeros((64, 128), F32) for _ in range(4)]
        for dx in range(2):
            x = 2 * x2 + dx
            prod = dot(lhs1, cols_of(x))
            for y in range(8):
                lanes = slice(y * 128, y * 128 + 128)
                pre = prod[64:128, lanes]
                if y > 0:
                    pre = pre + prod[0:64, (y - 1) * 128 : y * 128]
                if y < 7:
                    pre = pre + prod[128:192, (y + 1) * 128 : (y + 2) * 128]
                sig = jax.nn.sigmoid(pre)
                act = pre * sig
                slope[x, :, lanes] = sig + act * (1.0 - sig)
                total[y // 2] = total[y // 2] + act
        for h in range(2):
            hi, lo = halves(jnp.concatenate([total[2 * h], total[2 * h + 1]], axis=1))
            fpl[x2, :, h * 128 : h * 128 + 128] = (
                (dot(hi, pool1) + dot(lo, pool1)) * 0.125
            ).astype(BF).astype(F32)

    fs[0] = jnp.zeros((576, 256), BF)
    fs[5] = jnp.zeros((576, 256), BF)
    d2p[0] = jnp.zeros((128, 256), BF)
    d2p[5] = jnp.zeros((128, 256), BF)
    for x2 in range(4):
        plane = fpl[x2]
        for bc in range(9):
            fs[x2 + 1, bc * 64 : bc * 64 + 64, :] = roll_yz(plane, bc // 3 - 1, bc % 3 - 1).astype(BF)
    w2t = dot_nt(id128, w2s[...]).astype(BF)
    col = iota((64, 256), 1)
    spread2 = where_one(iota((64, 256), 0) == (col // 128) * 32 + (col % 64) // 2)
    col = iota((64, 256), 1)
    pool2 = where_one(iota((64, 256), 0) == (col // 128) * 32 + (col % 64) // 2)
    for x4 in range(2):
        cot = lax.select(x4 == s, co[...], cx[...])
        wide = dot(dot_nt(id128, cot).astype(BF), spread2) * 0.125
        total = jnp.zeros((128, 256), F32)
        for dx in range(2):
            x2 = 2 * x4 + dx
            rhs = jnp.concatenate([fs[x2], fs[x2 + 1], fs[x2 + 2]], axis=0)
            pre = dot(w2t, rhs)
            sig = jax.nn.sigmoid(pre)
            act = pre * sig
            total = total + act
            d2p[x2 + 1] = (wide * (sig + act * (1.0 - sig))).astype(BF)
        t2[x4] = total
    hi, lo = halves(t2[s])
    pooled_out[...] = ((dot_nt(pool2, hi) + dot_nt(pool2, lo)) * 0.125).astype(BF)

    lhs = jnp.concatenate([fs[p] for p in range(1, 5)], axis=1)
    rhs = jnp.concatenate(
        [jnp.concatenate([d2p[p + 1 - a] for p in range(1, 5)], axis=1) for a in range(3)], axis=0
    )
    prod = dot_nt(lhs, rhs) * factor_two
    for a in range(3):
        g2f[a * 576 : a * 576 + 576, :] = prod[:, a * 128 : a * 128 + 128]
    g2f[1728:1736, :] = jnp.zeros((8, 128), F32)

    spread1 = where_one(iota((128, 256), 0) == iota((128, 256), 1) // 2)
    dp[0] = jnp.zeros((64, 1280), BF)
    dp[9] = jnp.zeros((64, 1280), BF)
    for x in range(8):
        dp[x + 1, :, 0:128] = jnp.zeros((64, 128), BF)
        dp[x + 1, :, 1152:1280] = jnp.zeros((64, 128), BF)
    back = jnp.concatenate([w2s[a * 576 : a * 576 + 576, :] for a in range(3)], axis=1)
    for x2 in range(4):
        rhs = jnp.concatenate([d2p[x2 + 2], d2p[x2 + 1], d2p[x2]], axis=0)
        prod = dot(back, rhs)
        grad = prod[256:320]
        for bc in range(9):
            if bc != 4:
                grad = grad + roll_yz(prod[bc * 64 : bc * 64 + 64], 1 - bc // 3, 1 - bc % 3)
        grad = grad.astype(BF)
        for h in range(2):
            wide = dot(grad[:, h * 128 : h * 128 + 128], spread1) * 0.125
            for dx in range(2):
                for y in range(4):
                    at = (4 * h + y) * 128
                    part = wide[:, (y // 2) * 128 : (y // 2) * 128 + 128]
                    dp[2 * x2 + dx + 1, :, at + 128 : at + 256] = (
                        part * slope[2 * x2 + dx, :, at : at + 128]
                    ).astype(BF)

    prod = jnp.zeros((288, 192), F32)
    for x in range(8):
        rhs = jnp.concatenate([dp[x + 1, :, (2 - b) * 128 : (2 - b) * 128 + 1024] for b in range(3)], axis=0)
        prod = prod + dot_nt(cols_of(x), rhs)
    prod = prod * factor_one
    g1w[0:32, :] = jnp.zeros((32, 128), F32)
    g1w[896:904, :] = jnp.zeros((8, 128), F32)
    g1w[864:896, :] = jnp.zeros((32, 128), F32)
    for a in range(3):
        for b in range(3):
            block = prod[a * 96 : a * 96 + 96, b * 64 : b * 64 + 64]
            row = (a * 3 + b) * 96 + 32
            g1w[row : row + 96, 0:64] = block
            g1w[row - 27 : row + 69, 64:128] = block
    for parity in range(2):

        @pl.when(me % 2 == parity)
        def _():
            for d in range(16):
                k = jnp.bitwise_xor(me, d)
                ref = keep_out if d % 2 == parity else send_out
                place = (k // 2) % 2 * 4 + k // 4
                ref[place, 0:112, :] = g2f[108 * d : 108 * d + 112, :].astype(BF)
                ref[place, 112:144, :] = g1w[54 * d + 32 : 54 * d + 64, :].astype(BF)


def volume_kernel(pos, dp, w1, out, wd):
    s = pos[1]
    for ab in range(9):
        wd[:, ab * 64 : ab * 64 + 64] = w1[ab * 96 : ab * 96 + 96, :]
    lhs = wd[...]
    for p in range(4):
        x = 4 * s + p
        rhs = jnp.concatenate(
            [
                dp[x + 2 - a, :, (2 - b) * 128 : (2 - b) * 128 + 1024]
                for a in range(3)
                for b in range(3)
            ],
            axis=0,
        )
        prod = dot(lhs, rhs)
        for y in range(8):
            part = prod[:, y * 128 : y * 128 + 128]
            out[p, :, y * 128 : y * 128 + 128] = (
                part[32:64] + roll_z(part[0:32], -1) + roll_z(part[64:96], 1)
            ).astype(BF)


def fused_call(factor_one, factor_two, pos, v3, co, cx, near, far):
    return pl.pallas_call(
        functools.partial(fused_kernel, factor_one, factor_two),
        out_shape=(
            jax.ShapeDtypeStruct((64, 128), BF),
            jax.ShapeDtypeStruct((8, 144, 128), BF),
            jax.ShapeDtypeStruct((8, 144, 128), BF),
            jax.ShapeDtypeStruct((10, 64, 1280), BF),
            jax.ShapeDtypeStruct((864, 64), BF),
        ),
        in_specs=[SMEM] + [VMEM] * 5,
        out_specs=(VMEM,) * 5,
        scratch_shapes=[
            pltpu.VMEM((864, 64), F32),
            pltpu.VMEM((1728, 128), F32),
            pltpu.VMEM((1728, 128), BF),
            pltpu.VMEM((8, 64, 1024), F32),
            pltpu.VMEM((4, 64, 256), F32),
            pltpu.VMEM((6, 576, 256), BF),
            pltpu.VMEM((6, 128, 256), BF),
            pltpu.VMEM((2, 128, 256), F32),
            pltpu.VMEM((1736, 128), F32),
            pltpu.VMEM((904, 128), F32),
        ],
        compiler_params=pltpu.CompilerParams(vmem_limit_bytes=48 << 20),
        cost_estimate=pl.CostEstimate(flops=4_000_000_000, bytes_accessed=6_000_000, transcendentals=700_000),
        name="fused",
    )(pos, v3, co, cx, near, far)


def volume_call(pos, dp, w1):
    return pl.pallas_call(
        volume_kernel,
        out_shape=jax.ShapeDtypeStruct((4, 32, 1024), BF),
        in_specs=[SMEM, VMEM, VMEM],
        out_specs=VMEM,
        scratch_shapes=[pltpu.VMEM((96, 576), BF)],
        compiler_params=pltpu.CompilerParams(vmem_limit_bytes=16 << 20),
        cost_estimate=pl.CostEstimate(flops=1_000_000_000, bytes_accessed=3_000_000, transcendentals=0),
        name="volume",
    )(pos, dp, w1)


def fits(volumes, w_first, w_second, cotangent):
    return (
        lax.axis_size("dp") == 16
        and lax.axis_size("space") == 2
        and volumes.shape == (1, 32, 4, 8, 128)
        and w_first.shape == (54, 64)
        and w_second.shape == (108, 128)
        and cotangent.shape == (1, 128, 1, 2, 32)
    )


def swap(x, bit):
    return lax.ppermute(x, "dp", [(i, i ^ bit) for i in range(16)])


def plane_major(block):
    return jnp.transpose(block[0], (1, 0, 2, 3)).reshape(4, 32, 1024)


def paired(volumes, w_first, w_second, cotangent):
    count = 16 * 2 * (volumes.size // 32)
    factor_one, factor_two = float(count) ** (-0.5), float(count // 8) ** (-0.5)
    across_space = [(0, 1), (1, 0)]
    pos = jnp.stack([lax.axis_index("dp"), lax.axis_index("space")]).astype(jnp.int32)
    volumes_other = lax.ppermute(volumes, "space", across_space)
    cot = jnp.transpose(cotangent, (0, 2, 3, 4, 1)).reshape(64, 128)
    cot_other = lax.ppermute(cot, "space", across_space)
    shard = pack_call(w_first, w_second)
    pieces = [swap(shard, 4 * k) for k in range(1, 4)]
    along_z = jnp.stack([shard] + pieces)
    piece = swap(along_z, 2)
    along_y = jnp.concatenate([along_z, piece])
    across = swap(along_y, 1)
    own = plane_major(volumes)
    other = plane_major(volumes_other)
    moved = shift_call(pos, own, other)
    pooled, keep, send, delta, w_one = fused_call(
        factor_one, factor_two, pos, moved, cot, cot_other, along_y, across
    )
    got = swap(send, 1)
    part = (keep.astype(F32) + got.astype(F32)).astype(BF)
    got = swap(part[4:], 2)
    part = (part[:4].astype(F32) + got.astype(F32)).astype(BF)
    pieces = [swap(part[k], 4 * k) for k in range(1, 4)]
    share_one, share_two = finish_call(part, pieces)
    grad = volume_call(pos, delta, w_one)
    grad = jnp.transpose(grad.reshape(4, 32, 8, 128), (1, 0, 2, 3))[None]
    pooled = jnp.transpose(pooled.reshape(1, 1, 2, 32, 128), (0, 4, 1, 2, 3))
    return pooled, grad, share_one, share_two


def with_halo(block, sides, width):
    for axis, dim in sides:
        count = lax.axis_size(axis)
        forward = [(i, i + 1) for i in range(count - 1)]
        backward = [(target, source) for source, target in forward]
        low = lax.ppermute(
            lax.slice_in_dim(block, block.shape[dim] - width, None, axis=dim), axis, forward
        )
        high = lax.ppermute(lax.slice_in_dim(block, 0, width, axis=dim), axis, backward)
        block = jnp.concatenate([low, block, high], axis=dim)
    return block


def pad_sides(field):
    return jnp.pad(field, ((0, 0), (0, 0), (0, 0), (1, 1), (1, 1)))


def conv_forward(padded, weight):
    samples_here, in_width, depth_padded, extent_y, extent_z = padded.shape
    extent_x = depth_padded - 2
    out_width = weight.shape[1]
    framed = pad_sides(padded)
    kernel = weight.reshape(3, 3, 3, in_width, out_width)
    summed = jnp.zeros((samples_here, out_width, extent_x, extent_y, extent_z), jnp.float32)
    for along_x in range(3):
        for along_y in range(3):
            for along_z in range(3):
                window = framed[
                    :,
                    :,
                    along_x : along_x + extent_x,
                    along_y : along_y + extent_y,
                    along_z : along_z + extent_z,
                ]
                summed = summed + jnp.einsum(
                    "sixyz,io->soxyz",
                    window,
                    kernel[along_x, along_y, along_z],
                    preferred_element_type=jnp.float32,
                )
    return summed


def conv_input_grad(padded, weight, in_width):
    samples_here, out_width, depth_padded, extent_y, extent_z = padded.shape
    extent_x = depth_padded - 2
    framed = pad_sides(padded)
    kernel = weight.reshape(3, 3, 3, in_width, out_width)
    summed = jnp.zeros((samples_here, in_width, extent_x, extent_y, extent_z), jnp.float32)
    for along_x in range(3):
        for along_y in range(3):
            for along_z in range(3):
                window = framed[
                    :,
                    :,
                    2 - along_x : 2 - along_x + extent_x,
                    2 - along_y : 2 - along_y + extent_y,
                    2 - along_z : 2 - along_z + extent_z,
                ]
                summed = summed + jnp.einsum(
                    "soxyz,io->sixyz",
                    window,
                    kernel[along_x, along_y, along_z],
                    preferred_element_type=jnp.float32,
                )
    return summed


def conv_weight_grad(padded, grads):
    _, in_width, depth_padded, extent_y, extent_z = padded.shape
    extent_x = depth_padded - 2
    framed = pad_sides(padded)
    pieces = []
    for along_x in range(3):
        for along_y in range(3):
            for along_z in range(3):
                window = framed[
                    :,
                    :,
                    along_x : along_x + extent_x,
                    along_y : along_y + extent_y,
                    along_z : along_z + extent_z,
                ]
                pieces.append(
                    jnp.einsum("sixyz,soxyz->io", window, grads, preferred_element_type=jnp.float32)
                )
    return jnp.stack(pieces).reshape(27 * in_width, grads.shape[1])


def pooling(field):
    samples_here, width, extent_x, extent_y, extent_z = field.shape
    blocks = field.reshape(
        samples_here, width, extent_x // 2, 2, extent_y // 2, 2, extent_z // 2, 2
    )
    return jnp.mean(blocks, axis=(3, 5, 7))


def spread_up(field):
    samples_here, width, extent_x, extent_y, extent_z = field.shape
    blocks = jnp.broadcast_to(
        field[:, :, :, None, :, None, :, None],
        (samples_here, width, extent_x, 2, extent_y, 2, extent_z, 2),
    )
    return blocks.reshape(samples_here, width, 2 * extent_x, 2 * extent_y, 2 * extent_z)


def silu_slope(values):
    sigma = jax.nn.sigmoid(values)
    return sigma * (1.0 + values * (1.0 - sigma))


def general(volumes, w_first, w_second, cotangent):
    kernel_one, kernel_two = (
        lax.all_gather(w_first, "dp", axis=0, tiled=True),
        lax.all_gather(w_second, "dp", axis=0, tiled=True),
    )
    in_width = volumes.shape[1]
    mid_width = kernel_one.shape[1]
    count_one = lax.axis_size("dp") * lax.axis_size("space") * (volumes.size // in_width)
    factor_one = float(count_one) ** (-0.5)
    factor_two = float(count_one // 8) ** (-0.5)
    input_padded = with_halo(volumes, (("space", 2),), 1)
    first_pre = conv_forward(input_padded, kernel_one)
    first_pool = pooling(jax.nn.silu(first_pre)).astype(jnp.bfloat16)
    pool_padded = with_halo(first_pool, (("space", 2),), 1)
    second_pre = conv_forward(pool_padded, kernel_two)
    pooled = pooling(jax.nn.silu(second_pre)).astype(jnp.bfloat16)
    second_delta = (
        spread_up(cotangent.astype(jnp.float32)) * 0.125 * silu_slope(second_pre)
    ).astype(jnp.bfloat16)
    grad_two = conv_weight_grad(pool_padded, second_delta) * factor_two
    delta_padded = with_halo(second_delta, (("space", 2),), 1)
    pool_grad = conv_input_grad(delta_padded, kernel_two, mid_width).astype(jnp.bfloat16)
    first_delta = (spread_up(pool_grad.astype(jnp.float32)) * 0.125 * silu_slope(first_pre)).astype(
        jnp.bfloat16
    )
    grad_one = conv_weight_grad(input_padded, first_delta) * factor_one
    first_padded = with_halo(first_delta, (("space", 2),), 1)
    volume_grad = conv_input_grad(first_padded, kernel_one, in_width).astype(jnp.bfloat16)
    rows_one, rows_two = (
        lax.psum_scatter(
            grad_one.astype(jnp.bfloat16), "dp", scatter_dimension=0, tiled=True
        ).astype(jnp.float32),
        lax.psum_scatter(
            grad_two.astype(jnp.bfloat16), "dp", scatter_dimension=0, tiled=True
        ).astype(jnp.float32),
    )
    share_one, share_two = (
        lax.psum(rows_one.astype(jnp.bfloat16), "space").astype(jnp.float32),
        lax.psum(rows_two.astype(jnp.bfloat16), "space").astype(jnp.float32),
    )
    return (pooled, volume_grad, share_one, share_two)


def local(volumes, w_first, w_second, cotangent):
    if fits(volumes, w_first, w_second, cotangent):
        return paired(volumes, w_first, w_second, cotangent)
    return general(volumes, w_first, w_second, cotangent)


def solution(mesh):
    return jax.shard_map(
        local,
        mesh=mesh,
        in_specs=(
            P("dp", None, "space", None, None),
            P("dp", None),
            P("dp", None),
            P("dp", None, "space", None, None),
        ),
        out_specs=(
            P("dp", None, "space", None, None),
            P("dp", None, "space", None, None),
            P("dp", None),
            P("dp", None),
        ),
        check_vma=False,
    )
```

```python
import functools

import jax
import jax.numpy as jnp
from jax import lax
from jax.experimental import pallas as pl
from jax.experimental.pallas import tpu as pltpu
from jax.sharding import PartitionSpec as P


BF = jnp.bfloat16
F32 = jnp.float32
VMEM = pl.BlockSpec(memory_space=pltpu.VMEM)
SMEM = pl.BlockSpec(memory_space=pltpu.SMEM)


def dot(a, b):
    return jnp.dot(a, b, preferred_element_type=F32)


def dot_nt(a, b):
    return lax.dot_general(a, b, (((1,), (1,)), ((), ())), preferred_element_type=F32)


def iota(shape, dim):
    return lax.broadcasted_iota(jnp.int32, shape, dim)


def where_one(mask):
    return mask.astype(F32).astype(BF)


def eye(n):
    return where_one(iota((n, n), 0) == iota((n, n), 1))


def halves(x):
    hi = x.astype(BF)
    return hi, (x - hi.astype(F32)).astype(BF)


def roll_z(x, by):
    lane = iota(x.shape, 1)
    edge = 0 if by == 1 else 127
    return jnp.where(lane == edge, 0.0, pltpu.roll(x, by % 128, 1))


def roll_yz(x, db, dc):
    if db == 0 and dc == 0:
        return x
    lane = iota(x.shape, 1)
    y, z = lane // 64 + db, lane % 64 + dc
    inside = (y >= 0) & (y < 4) & (z >= 0) & (z < 64)
    return jnp.where(inside, pltpu.roll(x, (-(db * 64 + dc)) % 256, 1), 0.0)


def pack_kernel(first, second, out, wide, narrow, first_here, second_here, sems):
    copies = (
        pltpu.make_async_copy(first, first_here, sems.at[0]),
        pltpu.make_async_copy(second, second_here, sems.at[1]),
    )
    for copy in copies:
        copy.start()
    wide[...] = jnp.zeros(wide.shape, F32)
    for copy in copies:
        copy.wait()
    wide[0:108, :] = second_here[...].astype(F32)
    narrow[...] = first_here[...].astype(F32)
    wide[112:140, 0:64] = narrow[0:28, :]
    wide[112:138, 64:128] = narrow[28:54, :]
    out[...] = wide[...].astype(BF)


def pack_call(first, second):
    return pl.pallas_call(
        pack_kernel,
        out_shape=jax.ShapeDtypeStruct((144, 128), BF),
        in_specs=[pl.BlockSpec(memory_space=pltpu.HBM)] * 2,
        out_specs=VMEM,
        scratch_shapes=[
            pltpu.VMEM((144, 128), F32),
            pltpu.VMEM((54, 64), F32),
            pltpu.VMEM((54, 64), BF),
            pltpu.VMEM((108, 128), BF),
            pltpu.SemaphoreType.DMA((2,)),
        ],
        compiler_params=pltpu.CompilerParams(vmem_limit_bytes=2 << 20),
        cost_estimate=pl.CostEstimate(flops=40_000, bytes_accessed=80_000, transcendentals=0),
        name="pack",
    )(first, second)


def finish_kernel(kept, one, two, three, first, second, total):
    total[...] = (
        kept[0].astype(F32) + one[...].astype(F32) + two[...].astype(F32) + three[...].astype(F32)
    )
    second[...] = total[0:108, :]
    first[0:28, :] = total[112:140, 0:64]
    first[28:54, :] = total[112:138, 64:128]


def finish_call(kept, pieces):
    return pl.pallas_call(
        finish_kernel,
        out_shape=(
            jax.ShapeDtypeStruct((54, 64), F32),
            jax.ShapeDtypeStruct((108, 128), F32),
        ),
        in_specs=[VMEM] * 4,
        out_specs=(VMEM,) * 2,
        scratch_shapes=[pltpu.VMEM((144, 128), F32)],
        compiler_params=pltpu.CompilerParams(vmem_limit_bytes=2 << 20),
        cost_estimate=pl.CostEstimate(flops=80_000, bytes_accessed=300_000, transcendentals=0),
        name="finish",
    )(kept, *pieces)


def shift_kernel(pos, own, other, out):
    s = pos[1]
    out[0] = jnp.zeros((96, 1024), BF)
    out[9] = jnp.zeros((96, 1024), BF)
    for p in range(4):
        for block, place in ((own, 4 * s + 1 + p), (other, 4 * (1 - s) + 1 + p)):
            out[place, 32:64, :] = block[p]
            for y in range(8):
                lanes = slice(y * 128, y * 128 + 128)
                line = block[p, :, lanes].astype(F32)
                out[place, 0:32, lanes] = roll_z(line, 1).astype(BF)
                out[place, 64:96, lanes] = roll_z(line, -1).astype(BF)


def shift_call(pos, own, other):
    return pl.pallas_call(
        shift_kernel,
        out_shape=jax.ShapeDtypeStruct((10, 96, 1024), BF),
        in_specs=[SMEM, VMEM, VMEM],
        out_specs=VMEM,
        compiler_params=pltpu.CompilerParams(vmem_limit_bytes=8 << 20),
        cost_estimate=pl.CostEstimate(flops=600_000, bytes_accessed=2_500_000, transcendentals=0),
        name="shift",
    )(pos, own, other)


def unpack_weights(me, near, far, w1s, w2s):
    for d in range(16):
        k = jnp.bitwise_xor(me, d)
        place = (k // 2) % 2 * 4 + k // 4
        blk = lax.select(k % 2 == 0, near[place], far[place])
        w2s[108 * d : 108 * d + 108, :] = blk[0:108]
        w1s[54 * d : 54 * d + 28, :] = blk[112:140, 0:64]
        w1s[54 * d + 28 : 54 * d + 54, :] = blk[112:138, 64:128]


def fused_kernel(
    factor_one, factor_two,
    pos, v3, co, cx, near, far,
    pooled_out, wire_out, dp, w1_out,
    w2s, slope, fpl, fs, d2p, t2, g2s, g1s, acc1,
):
    me, s = pos[0], pos[1]
    unpack_weights(me, near, far, w1_out, w2s)
    id64, id128 = eye(64), eye(128)
    lhs1 = jnp.concatenate(
        [
            dot_nt(
                id64,
                jnp.concatenate(
                    [w1_out[(a * 3 + b) * 96 : (a * 3 + b) * 96 + 96, :] for a in range(3)], axis=0
                ),
            ).astype(BF)
            for b in range(3)
        ],
        axis=0,
    )
    pool1 = where_one(iota((256, 128), 0) // 2 == iota((256, 128), 1))

    def cols_of(x):
        return jnp.concatenate([v3[x], v3[x + 1], v3[x + 2]], axis=0)

    for x2 in range(4):
        total = [jnp.zeros((64, 128), F32) for _ in range(4)]
        for dx in range(2):
            x = 2 * x2 + dx
            prod = dot(lhs1, cols_of(x))
            for y in range(8):
                lanes = slice(y * 128, y * 128 + 128)
                pre = prod[64:128, lanes]
                if y > 0:
                    pre = pre + prod[0:64, (y - 1) * 128 : y * 128]
                if y < 7:
                    pre = pre + prod[128:192, (y + 1) * 128 : (y + 2) * 128]
                sig = jax.nn.sigmoid(pre)
                act = pre * sig
                slope[x, :, lanes] = sig + act * (1.0 - sig)
                total[y // 2] = total[y // 2] + act
        for h in range(2):
            hi, lo = halves(jnp.concatenate([total[2 * h], total[2 * h + 1]], axis=1))
            fpl[x2, :, h * 128 : h * 128 + 128] = (
                (dot(hi, pool1) + dot(lo, pool1)) * 0.125
            ).astype(BF).astype(F32)

    fs[0] = jnp.zeros((576, 256), BF)
    fs[5] = jnp.zeros((576, 256), BF)
    d2p[0] = jnp.zeros((128, 256), BF)
    d2p[5] = jnp.zeros((128, 256), BF)
    for x2 in range(4):
        plane = fpl[x2]
        for bc in range(9):
            fs[x2 + 1, bc * 64 : bc * 64 + 64, :] = roll_yz(plane, bc // 3 - 1, bc % 3 - 1).astype(BF)
    w2t = dot_nt(id128, w2s[...]).astype(BF)
    col = iota((64, 256), 1)
    spread2 = where_one(iota((64, 256), 0) == (col // 128) * 32 + (col % 64) // 2)
    col = iota((64, 256), 1)
    pool2 = where_one(iota((64, 256), 0) == (col // 128) * 32 + (col % 64) // 2)
    for x4 in range(2):
        cot = lax.select(x4 == s, co[...], cx[...])
        wide = dot(dot_nt(id128, cot).astype(BF), spread2) * 0.125
        total = jnp.zeros((128, 256), F32)
        for dx in range(2):
            x2 = 2 * x4 + dx
            rhs = jnp.concatenate([fs[x2], fs[x2 + 1], fs[x2 + 2]], axis=0)
            pre = dot(w2t, rhs)
            sig = jax.nn.sigmoid(pre)
            act = pre * sig
            total = total + act
            d2p[x2 + 1] = (wide * (sig + act * (1.0 - sig))).astype(BF)
        t2[x4] = total
    hi, lo = halves(t2[s])
    pooled_out[...] = ((dot_nt(pool2, hi) + dot_nt(pool2, lo)) * 0.125).astype(BF)

    lhs = jnp.concatenate([fs[p] for p in range(1, 5)], axis=1)
    for some in ((0, 1), (2,)):
        rhs = jnp.concatenate(
            [jnp.concatenate([d2p[p + 1 - a] for p in range(1, 5)], axis=1) for a in some], axis=0
        )
        prod = dot_nt(lhs, rhs) * factor_two
        for n, a in enumerate(some):
            g2s[a * 576 : a * 576 + 576, :] = prod[:, n * 128 : n * 128 + 128].astype(BF)
    g2s[1728:1744, :] = jnp.zeros((16, 128), BF)

    spread1 = where_one(iota((128, 256), 0) == iota((128, 256), 1) // 2)
    dp[0] = jnp.zeros((64, 1280), BF)
    dp[9] = jnp.zeros((64, 1280), BF)
    for x in range(8):
        dp[x + 1, :, 0:128] = jnp.zeros((64, 128), BF)
        dp[x + 1, :, 1152:1280] = jnp.zeros((64, 128), BF)
    back = jnp.concatenate([w2s[a * 576 : a * 576 + 576, :] for a in range(3)], axis=1)
    rhs = jnp.concatenate(
        [jnp.concatenate([d2p[x2 + 2 - a] for x2 in range(4)], axis=1) for a in range(3)], axis=0
    )
    spread_all = dot(back, rhs)
    for x2 in range(4):
        prod = spread_all[:, x2 * 256 : x2 * 256 + 256]
        grad = prod[256:320]
        for bc in range(9):
            if bc != 4:
                grad = grad + roll_yz(prod[bc * 64 : bc * 64 + 64], 1 - bc // 3, 1 - bc % 3)
        grad = grad.astype(BF)
        for h in range(2):
            wide = dot(grad[:, h * 128 : h * 128 + 128], spread1) * 0.125
            for dx in range(2):
                for y in range(4):
                    at = (4 * h + y) * 128
                    part = wide[:, (y // 2) * 128 : (y // 2) * 128 + 128]
                    dp[2 * x2 + dx + 1, :, at + 128 : at + 256] = (
                        part * slope[2 * x2 + dx, :, at : at + 128]
                    ).astype(BF)

    acc1[...] = jnp.zeros(acc1.shape, F32)

    def first_grads(i, carry):
        for n in range(4):
            x = 4 * i + n
            rhs = jnp.concatenate(
                [dp[x + 1, :, (2 - b) * 128 : (2 - b) * 128 + 1024] for b in range(3)], axis=0
            )
            acc1[n % 2] += dot_nt(cols_of(x), rhs)
        return carry

    lax.fori_loop(0, 2, first_grads, 0)
    prod = (acc1[0] + acc1[1]) * factor_one
    g1s[0:32, :] = jnp.zeros((32, 128), BF)
    g1s[864:912, :] = jnp.zeros((48, 128), BF)
    for a in range(3):
        for b in range(3):
            block = prod[a * 96 : a * 96 + 96, b * 64 : b * 64 + 64].astype(BF)
            row = (a * 3 + b) * 96 + 32
            g1s[row : row + 96, 0:64] = block
            g1s[row - 28 : row + 68, 64:128] = block
    for d in range(16):
        k = jnp.bitwise_xor(me, d)
        place = k % 2 * 8 + (k // 2) % 2 * 4 + k // 4
        wire_out[place, 0:112, :] = g2s[108 * d : 108 * d + 112, :]
        wire_out[place, 112:144, :] = g1s[54 * d + 32 : 54 * d + 64, :]


def volume_kernel(pos, dp, w1, out, wd):
    s = pos[1]
    for ab in range(9):
        wd[:, ab * 64 : ab * 64 + 64] = w1[ab * 96 : ab * 96 + 96, :]
    lhs = wd[...]
    for p in range(4):
        x = 4 * s + p
        rhs = jnp.concatenate(
            [
                dp[x + 2 - a, :, (2 - b) * 128 : (2 - b) * 128 + 1024]
                for a in range(3)
                for b in range(3)
            ],
            axis=0,
        )
        prod = dot(lhs, rhs)
        for y in range(8):
            part = prod[:, y * 128 : y * 128 + 128]
            out[p, :, y * 128 : y * 128 + 128] = (
                part[32:64] + roll_z(part[0:32], -1) + roll_z(part[64:96], 1)
            ).astype(BF)


def fused_call(factor_one, factor_two, pos, v3, co, cx, near, far):
    return pl.pallas_call(
        functools.partial(fused_kernel, factor_one, factor_two),
        out_shape=(
            jax.ShapeDtypeStruct((64, 128), BF),
            jax.ShapeDtypeStruct((16, 144, 128), BF),
            jax.ShapeDtypeStruct((10, 64, 1280), BF),
            jax.ShapeDtypeStruct((864, 64), BF),
        ),
        in_specs=[SMEM] + [VMEM] * 5,
        out_specs=(VMEM,) * 4,
        scratch_shapes=[
            pltpu.VMEM((1728, 128), BF),
            pltpu.VMEM((8, 64, 1024), F32),
            pltpu.VMEM((4, 64, 256), F32),
            pltpu.VMEM((6, 576, 256), BF),
            pltpu.VMEM((6, 128, 256), BF),
            pltpu.VMEM((2, 128, 256), F32),
            pltpu.VMEM((1744, 128), BF),
            pltpu.VMEM((912, 128), BF),
            pltpu.VMEM((2, 288, 192), F32),
        ],
        compiler_params=pltpu.CompilerParams(vmem_limit_bytes=48 << 20),
        cost_estimate=pl.CostEstimate(flops=4_000_000_000, bytes_accessed=6_000_000, transcendentals=700_000),
        name="fused",
    )(pos, v3, co, cx, near, far)


def volume_call(pos, dp, w1):
    return pl.pallas_call(
        volume_kernel,
        out_shape=jax.ShapeDtypeStruct((4, 32, 1024), BF),
        in_specs=[SMEM, VMEM, VMEM],
        out_specs=VMEM,
        scratch_shapes=[pltpu.VMEM((96, 576), BF)],
        compiler_params=pltpu.CompilerParams(vmem_limit_bytes=16 << 20),
        cost_estimate=pl.CostEstimate(flops=1_000_000_000, bytes_accessed=3_000_000, transcendentals=0),
        name="volume",
    )(pos, dp, w1)


def fits(volumes, w_first, w_second, cotangent):
    return (
        lax.axis_size("dp") == 16
        and lax.axis_size("space") == 2
        and volumes.shape == (1, 32, 4, 8, 128)
        and w_first.shape == (54, 64)
        and w_second.shape == (108, 128)
        and cotangent.shape == (1, 128, 1, 2, 32)
    )


def swap(x, bit):
    return lax.ppermute(x, "dp", [(i, i ^ bit) for i in range(16)])


def plane_major(block):
    return jnp.transpose(block[0], (1, 0, 2, 3)).reshape(4, 32, 1024)


def paired(volumes, w_first, w_second, cotangent):
    count = 16 * 2 * (volumes.size // 32)
    factor_one, factor_two = float(count) ** (-0.5), float(count // 8) ** (-0.5)
    across_space = [(0, 1), (1, 0)]
    pos = jnp.stack([lax.axis_index("dp"), lax.axis_index("space")]).astype(jnp.int32)
    volumes_other = lax.ppermute(volumes, "space", across_space)
    cot = jnp.transpose(cotangent, (0, 2, 3, 4, 1)).reshape(64, 128)
    cot_other = lax.ppermute(cot, "space", across_space)
    shard = pack_call(w_first, w_second)
    pieces = [swap(shard, 4 * k) for k in range(1, 4)]
    along_z = jnp.stack([shard] + pieces)
    piece = swap(along_z, 2)
    along_y = jnp.concatenate([along_z, piece])
    across = swap(along_y, 1)
    own = plane_major(volumes)
    other = plane_major(volumes_other)
    moved = shift_call(pos, own, other)
    pooled, wire, delta, w_one = fused_call(
        factor_one, factor_two, pos, moved, cot, cot_other, along_y, across
    )
    got = swap(wire[8:], 1)
    part = (wire[:8].astype(F32) + got.astype(F32)).astype(BF)
    got = swap(part[4:], 2)
    part = (part[:4].astype(F32) + got.astype(F32)).astype(BF)
    pieces = [swap(part[k], 4 * k) for k in range(1, 4)]
    share_one, share_two = finish_call(part, pieces)
    grad = volume_call(pos, delta, w_one)
    grad = jnp.transpose(grad.reshape(4, 32, 8, 128), (1, 0, 2, 3))[None]
    pooled = jnp.transpose(pooled.reshape(1, 1, 2, 32, 128), (0, 4, 1, 2, 3))
    return pooled, grad, share_one, share_two


def with_halo(block, sides, width):
    for axis, dim in sides:
        count = lax.axis_size(axis)
        forward = [(i, i + 1) for i in range(count - 1)]
        backward = [(target, source) for source, target in forward]
        low = lax.ppermute(
            lax.slice_in_dim(block, block.shape[dim] - width, None, axis=dim), axis, forward
        )
        high = lax.ppermute(lax.slice_in_dim(block, 0, width, axis=dim), axis, backward)
        block = jnp.concatenate([low, block, high], axis=dim)
    return block


def pad_sides(field):
    return jnp.pad(field, ((0, 0), (0, 0), (0, 0), (1, 1), (1, 1)))


def conv_forward(padded, weight):
    samples_here, in_width, depth_padded, extent_y, extent_z = padded.shape
    extent_x = depth_padded - 2
    out_width = weight.shape[1]
    framed = pad_sides(padded)
    kernel = weight.reshape(3, 3, 3, in_width, out_width)
    summed = jnp.zeros((samples_here, out_width, extent_x, extent_y, extent_z), jnp.float32)
    for along_x in range(3):
        for along_y in range(3):
            for along_z in range(3):
                window = framed[
                    :,
                    :,
                    along_x : along_x + extent_x,
                    along_y : along_y + extent_y,
                    along_z : along_z + extent_z,
                ]
                summed = summed + jnp.einsum(
                    "sixyz,io->soxyz",
                    window,
                    kernel[along_x, along_y, along_z],
                    preferred_element_type=jnp.float32,
                )
    return summed


def conv_input_grad(padded, weight, in_width):
    samples_here, out_width, depth_padded, extent_y, extent_z = padded.shape
    extent_x = depth_padded - 2
    framed = pad_sides(padded)
    kernel = weight.reshape(3, 3, 3, in_width, out_width)
    summed = jnp.zeros((samples_here, in_width, extent_x, extent_y, extent_z), jnp.float32)
    for along_x in range(3):
        for along_y in range(3):
            for along_z in range(3):
                window = framed[
                    :,
                    :,
                    2 - along_x : 2 - along_x + extent_x,
                    2 - along_y : 2 - along_y + extent_y,
                    2 - along_z : 2 - along_z + extent_z,
                ]
                summed = summed + jnp.einsum(
                    "soxyz,io->sixyz",
                    window,
                    kernel[along_x, along_y, along_z],
                    preferred_element_type=jnp.float32,
                )
    return summed


def conv_weight_grad(padded, grads):
    _, in_width, depth_padded, extent_y, extent_z = padded.shape
    extent_x = depth_padded - 2
    framed = pad_sides(padded)
    pieces = []
    for along_x in range(3):
        for along_y in range(3):
            for along_z in range(3):
                window = framed[
                    :,
                    :,
                    along_x : along_x + extent_x,
                    along_y : along_y + extent_y,
                    along_z : along_z + extent_z,
                ]
                pieces.append(
                    jnp.einsum("sixyz,soxyz->io", window, grads, preferred_element_type=jnp.float32)
                )
    return jnp.stack(pieces).reshape(27 * in_width, grads.shape[1])


def pooling(field):
    samples_here, width, extent_x, extent_y, extent_z = field.shape
    blocks = field.reshape(
        samples_here, width, extent_x // 2, 2, extent_y // 2, 2, extent_z // 2, 2
    )
    return jnp.mean(blocks, axis=(3, 5, 7))


def spread_up(field):
    samples_here, width, extent_x, extent_y, extent_z = field.shape
    blocks = jnp.broadcast_to(
        field[:, :, :, None, :, None, :, None],
        (samples_here, width, extent_x, 2, extent_y, 2, extent_z, 2),
    )
    return blocks.reshape(samples_here, width, 2 * extent_x, 2 * extent_y, 2 * extent_z)


def silu_slope(values):
    sigma = jax.nn.sigmoid(values)
    return sigma * (1.0 + values * (1.0 - sigma))


def general(volumes, w_first, w_second, cotangent):
    kernel_one, kernel_two = (
        lax.all_gather(w_first, "dp", axis=0, tiled=True),
        lax.all_gather(w_second, "dp", axis=0, tiled=True),
    )
    in_width = volumes.shape[1]
    mid_width = kernel_one.shape[1]
    count_one = lax.axis_size("dp") * lax.axis_size("space") * (volumes.size // in_width)
    factor_one = float(count_one) ** (-0.5)
    factor_two = float(count_one // 8) ** (-0.5)
    input_padded = with_halo(volumes, (("space", 2),), 1)
    first_pre = conv_forward(input_padded, kernel_one)
    first_pool = pooling(jax.nn.silu(first_pre)).astype(jnp.bfloat16)
    pool_padded = with_halo(first_pool, (("space", 2),), 1)
    second_pre = conv_forward(pool_padded, kernel_two)
    pooled = pooling(jax.nn.silu(second_pre)).astype(jnp.bfloat16)
    second_delta = (
        spread_up(cotangent.astype(jnp.float32)) * 0.125 * silu_slope(second_pre)
    ).astype(jnp.bfloat16)
    grad_two = conv_weight_grad(pool_padded, second_delta) * factor_two
    delta_padded = with_halo(second_delta, (("space", 2),), 1)
    pool_grad = conv_input_grad(delta_padded, kernel_two, mid_width).astype(jnp.bfloat16)
    first_delta = (spread_up(pool_grad.astype(jnp.float32)) * 0.125 * silu_slope(first_pre)).astype(
        jnp.bfloat16
    )
    grad_one = conv_weight_grad(input_padded, first_delta) * factor_one
    first_padded = with_halo(first_delta, (("space", 2),), 1)
    volume_grad = conv_input_grad(first_padded, kernel_one, in_width).astype(jnp.bfloat16)
    rows_one, rows_two = (
        lax.psum_scatter(
            grad_one.astype(jnp.bfloat16), "dp", scatter_dimension=0, tiled=True
        ).astype(jnp.float32),
        lax.psum_scatter(
            grad_two.astype(jnp.bfloat16), "dp", scatter_dimension=0, tiled=True
        ).astype(jnp.float32),
    )
    share_one, share_two = (
        lax.psum(rows_one.astype(jnp.bfloat16), "space").astype(jnp.float32),
        lax.psum(rows_two.astype(jnp.bfloat16), "space").astype(jnp.float32),
    )
    return (pooled, volume_grad, share_one, share_two)


def local(volumes, w_first, w_second, cotangent):
    if fits(volumes, w_first, w_second, cotangent):
        return paired(volumes, w_first, w_second, cotangent)
    return general(volumes, w_first, w_second, cotangent)


def solution(mesh):
    return jax.shard_map(
        local,
        mesh=mesh,
        in_specs=(
            P("dp", None, "space", None, None),
            P("dp", None),
            P("dp", None),
            P("dp", None, "space", None, None),
        ),
        out_specs=(
            P("dp", None, "space", None, None),
            P("dp", None, "space", None, None),
            P("dp", None),
            P("dp", None),
        ),
        check_vma=False,
    )
```

```python
import functools

import jax
import jax.numpy as jnp
from jax import lax
from jax.experimental import pallas as pl
from jax.experimental.pallas import tpu as pltpu
from jax.sharding import PartitionSpec as P


BF = jnp.bfloat16
F32 = jnp.float32
VMEM = pl.BlockSpec(memory_space=pltpu.VMEM)
SMEM = pl.BlockSpec(memory_space=pltpu.SMEM)


def dot(a, b):
    return jnp.dot(a, b, preferred_element_type=F32)


def dot_nt(a, b):
    return lax.dot_general(a, b, (((1,), (1,)), ((), ())), preferred_element_type=F32)


def iota(shape, dim):
    return lax.broadcasted_iota(jnp.int32, shape, dim)


def where_one(mask):
    return mask.astype(F32).astype(BF)


def eye(n):
    return where_one(iota((n, n), 0) == iota((n, n), 1))


def halves(x):
    hi = x.astype(BF)
    return hi, (x - hi.astype(F32)).astype(BF)


def roll_z(x, by):
    lane = iota(x.shape, 1)
    edge = 0 if by == 1 else 127
    return jnp.where(lane == edge, 0.0, pltpu.roll(x, by % 128, 1))


def roll_yz(x, db, dc):
    if db == 0 and dc == 0:
        return x
    lane = iota(x.shape, 1)
    y, z = lane // 64 + db, lane % 64 + dc
    inside = (y >= 0) & (y < 4) & (z >= 0) & (z < 64)
    return jnp.where(inside, pltpu.roll(x, (-(db * 64 + dc)) % 256, 1), 0.0)


def pack_kernel(first, second, out, wide, narrow, first_here, second_here, sems):
    copies = (
        pltpu.make_async_copy(first, first_here, sems.at[0]),
        pltpu.make_async_copy(second, second_here, sems.at[1]),
    )
    for copy in copies:
        copy.start()
    wide[...] = jnp.zeros(wide.shape, F32)
    for copy in copies:
        copy.wait()
    wide[0:108, :] = second_here[...].astype(F32)
    narrow[...] = first_here[...].astype(F32)
    wide[112:140, 0:64] = narrow[0:28, :]
    wide[112:138, 64:128] = narrow[28:54, :]
    out[...] = wide[...].astype(BF)


def pack_call(first, second):
    return pl.pallas_call(
        pack_kernel,
        out_shape=jax.ShapeDtypeStruct((144, 128), BF),
        in_specs=[pl.BlockSpec(memory_space=pltpu.HBM)] * 2,
        out_specs=VMEM,
        scratch_shapes=[
            pltpu.VMEM((144, 128), F32),
            pltpu.VMEM((54, 64), F32),
            pltpu.VMEM((54, 64), BF),
            pltpu.VMEM((108, 128), BF),
            pltpu.SemaphoreType.DMA((2,)),
        ],
        compiler_params=pltpu.CompilerParams(vmem_limit_bytes=2 << 20),
        cost_estimate=pl.CostEstimate(flops=40_000, bytes_accessed=80_000, transcendentals=0),
        name="pack",
    )(first, second)


def finish_kernel(wire, crossed, beside, one, two, three, first, second, total):
    total[...] = wire[0].astype(F32) + crossed[0].astype(F32) + beside[...].astype(F32)
    total[...] += one[...].astype(F32) + two[...].astype(F32) + three[...].astype(F32)
    second[...] = total[0:108, :]
    first[0:28, :] = total[112:140, 0:64]
    first[28:54, :] = total[112:138, 64:128]


def finish_call(wire, crossed, beside, pieces):
    return pl.pallas_call(
        finish_kernel,
        out_shape=(
            jax.ShapeDtypeStruct((54, 64), F32),
            jax.ShapeDtypeStruct((108, 128), F32),
        ),
        in_specs=[VMEM] * 6,
        out_specs=(VMEM,) * 2,
        scratch_shapes=[pltpu.VMEM((144, 128), F32)],
        compiler_params=pltpu.CompilerParams(vmem_limit_bytes=4 << 20),
        cost_estimate=pl.CostEstimate(flops=120_000, bytes_accessed=300_000, transcendentals=0),
        name="finish",
    )(wire, crossed, beside, *pieces)


def shift_kernel(pos, own, other, out):
    s = pos[1]
    out[0] = jnp.zeros((96, 1024), BF)
    out[9] = jnp.zeros((96, 1024), BF)
    for p in range(4):
        for block, place in ((own, 4 * s + 1 + p), (other, 4 * (1 - s) + 1 + p)):
            out[place, 32:64, :] = block[p]
            for y in range(8):
                lanes = slice(y * 128, y * 128 + 128)
                line = block[p, :, lanes].astype(F32)
                out[place, 0:32, lanes] = roll_z(line, 1).astype(BF)
                out[place, 64:96, lanes] = roll_z(line, -1).astype(BF)


def shift_call(pos, own, other):
    return pl.pallas_call(
        shift_kernel,
        out_shape=jax.ShapeDtypeStruct((10, 96, 1024), BF),
        in_specs=[SMEM, VMEM, VMEM],
        out_specs=VMEM,
        compiler_params=pltpu.CompilerParams(vmem_limit_bytes=8 << 20),
        cost_estimate=pl.CostEstimate(flops=600_000, bytes_accessed=2_500_000, transcendentals=0),
        name="shift",
    )(pos, own, other)


def unpack_weights(me, near, far, w1s, w2s):
    for d in range(16):
        k = jnp.bitwise_xor(me, d)
        place = (k // 2) % 2 * 4 + k // 4
        blk = lax.select(k % 2 == 0, near[place], far[place])
        w2s[108 * d : 108 * d + 108, :] = blk[0:108]
        w1s[54 * d : 54 * d + 28, :] = blk[112:140, 0:64]
        w1s[54 * d + 28 : 54 * d + 54, :] = blk[112:138, 64:128]


def fused_kernel(
    factor_one, factor_two,
    pos, v3, co, cx, near, far,
    pooled_out, wire_out, dp, w1_out,
    w2s, slope, fpl, fs, d2p, t2, g2s, g1s, acc1,
):
    me, s = pos[0], pos[1]
    unpack_weights(me, near, far, w1_out, w2s)
    id64, id128 = eye(64), eye(128)
    lhs1 = jnp.concatenate(
        [
            dot_nt(
                id64,
                jnp.concatenate(
                    [w1_out[(a * 3 + b) * 96 : (a * 3 + b) * 96 + 96, :] for a in range(3)], axis=0
                ),
            ).astype(BF)
            for b in range(3)
        ],
        axis=0,
    )
    pool1 = where_one(iota((256, 128), 0) // 2 == iota((256, 128), 1))

    def cols_of(x):
        return jnp.concatenate([v3[x], v3[x + 1], v3[x + 2]], axis=0)

    for x2 in range(4):
        total = [jnp.zeros((64, 128), F32) for _ in range(4)]
        for dx in range(2):
            x = 2 * x2 + dx
            prod = dot(lhs1, cols_of(x))
            for y in range(8):
                lanes = slice(y * 128, y * 128 + 128)
                pre = prod[64:128, lanes]
                if y > 0:
                    pre = pre + prod[0:64, (y - 1) * 128 : y * 128]
                if y < 7:
                    pre = pre + prod[128:192, (y + 1) * 128 : (y + 2) * 128]
                sig = jax.nn.sigmoid(pre)
                act = pre * sig
                slope[x, :, lanes] = sig + act * (1.0 - sig)
                total[y // 2] = total[y // 2] + act
        for h in range(2):
            hi, lo = halves(jnp.concatenate([total[2 * h], total[2 * h + 1]], axis=1))
            fpl[x2, :, h * 128 : h * 128 + 128] = (
                (dot(hi, pool1) + dot(lo, pool1)) * 0.125
            ).astype(BF).astype(F32)

    fs[0] = jnp.zeros((576, 256), BF)
    fs[5] = jnp.zeros((576, 256), BF)
    d2p[0] = jnp.zeros((128, 256), BF)
    d2p[5] = jnp.zeros((128, 256), BF)
    for x2 in range(4):
        plane = fpl[x2]
        for bc in range(9):
            fs[x2 + 1, bc * 64 : bc * 64 + 64, :] = roll_yz(plane, bc // 3 - 1, bc % 3 - 1).astype(BF)
    w2t = dot_nt(id128, w2s[...]).astype(BF)
    col = iota((64, 256), 1)
    spread2 = where_one(iota((64, 256), 0) == (col // 128) * 32 + (col % 64) // 2)
    col = iota((64, 256), 1)
    pool2 = where_one(iota((64, 256), 0) == (col // 128) * 32 + (col % 64) // 2)
    for x4 in range(2):
        cot = lax.select(x4 == s, co[...], cx[...])
        wide = dot(dot_nt(id128, cot).astype(BF), spread2) * 0.125
        total = jnp.zeros((128, 256), F32)
        for dx in range(2):
            x2 = 2 * x4 + dx
            rhs = jnp.concatenate([fs[x2], fs[x2 + 1], fs[x2 + 2]], axis=0)
            pre = dot(w2t, rhs)
            sig = jax.nn.sigmoid(pre)
            act = pre * sig
            total = total + act
            d2p[x2 + 1] = (wide * (sig + act * (1.0 - sig))).astype(BF)
        t2[x4] = total
    hi, lo = halves(t2[s])
    pooled_out[...] = ((dot_nt(pool2, hi) + dot_nt(pool2, lo)) * 0.125).astype(BF)

    lhs = jnp.concatenate([fs[p] for p in range(1, 5)], axis=1)
    for some in ((0, 1), (2,)):
        rhs = jnp.concatenate(
            [jnp.concatenate([d2p[p + 1 - a] for p in range(1, 5)], axis=1) for a in some], axis=0
        )
        prod = dot_nt(lhs, rhs) * factor_two
        for n, a in enumerate(some):
            g2s[a * 576 : a * 576 + 576, :] = prod[:, n * 128 : n * 128 + 128].astype(BF)
    g2s[1728:1744, :] = jnp.zeros((16, 128), BF)

    spread1 = where_one(iota((128, 256), 0) == iota((128, 256), 1) // 2)
    dp[0] = jnp.zeros((64, 1280), BF)
    dp[9] = jnp.zeros((64, 1280), BF)
    for x in range(8):
        dp[x + 1, :, 0:128] = jnp.zeros((64, 128), BF)
        dp[x + 1, :, 1152:1280] = jnp.zeros((64, 128), BF)
    back = jnp.concatenate([w2s[a * 576 : a * 576 + 576, :] for a in range(3)], axis=1)
    rhs = jnp.concatenate(
        [jnp.concatenate([d2p[x2 + 2 - a] for x2 in range(4)], axis=1) for a in range(3)], axis=0
    )
    spread_all = dot(back, rhs)
    for x2 in range(4):
        prod = spread_all[:, x2 * 256 : x2 * 256 + 256]
        grad = prod[256:320]
        for bc in range(9):
            if bc != 4:
                grad = grad + roll_yz(prod[bc * 64 : bc * 64 + 64], 1 - bc // 3, 1 - bc % 3)
        grad = grad.astype(BF)
        for h in range(2):
            wide = dot(grad[:, h * 128 : h * 128 + 128], spread1) * 0.125
            for dx in range(2):
                for y in range(4):
                    at = (4 * h + y) * 128
                    part = wide[:, (y // 2) * 128 : (y // 2) * 128 + 128]
                    dp[2 * x2 + dx + 1, :, at + 128 : at + 256] = (
                        part * slope[2 * x2 + dx, :, at : at + 128]
                    ).astype(BF)

    acc1[...] = jnp.zeros(acc1.shape, F32)

    def first_grads(i, carry):
        for n in range(4):
            x = 4 * i + n
            rhs = jnp.concatenate(
                [dp[x + 1, :, (2 - b) * 128 : (2 - b) * 128 + 1024] for b in range(3)], axis=0
            )
            acc1[n % 2] += dot_nt(cols_of(x), rhs)
        return carry

    lax.fori_loop(0, 2, first_grads, 0)
    prod = (acc1[0] + acc1[1]) * factor_one
    g1s[0:32, :] = jnp.zeros((32, 128), BF)
    g1s[864:912, :] = jnp.zeros((48, 128), BF)
    for a in range(3):
        for b in range(3):
            block = prod[a * 96 : a * 96 + 96, b * 64 : b * 64 + 64].astype(BF)
            row = (a * 3 + b) * 96 + 32
            g1s[row : row + 96, 0:64] = block
            g1s[row - 28 : row + 68, 64:128] = block
    for d in range(16):
        k = jnp.bitwise_xor(me, d)
        place = k % 2 * 8 + (k // 2) % 2 * 4 + k // 4
        wire_out[place, 0:112, :] = g2s[108 * d : 108 * d + 112, :]
        wire_out[place, 112:144, :] = g1s[54 * d + 32 : 54 * d + 64, :]


def volume_kernel(pos, dp, w1, out, wd):
    s = pos[1]
    for ab in range(9):
        wd[:, ab * 64 : ab * 64 + 64] = w1[ab * 96 : ab * 96 + 96, :]
    lhs = wd[...]
    for p in range(4):
        x = 4 * s + p
        rhs = jnp.concatenate(
            [
                dp[x + 2 - a, :, (2 - b) * 128 : (2 - b) * 128 + 1024]
                for a in range(3)
                for b in range(3)
            ],
            axis=0,
        )
        prod = dot(lhs, rhs)
        for y in range(8):
            part = prod[:, y * 128 : y * 128 + 128]
            out[p, :, y * 128 : y * 128 + 128] = (
                part[32:64] + roll_z(part[0:32], -1) + roll_z(part[64:96], 1)
            ).astype(BF)


def fused_call(factor_one, factor_two, pos, v3, co, cx, near, far):
    return pl.pallas_call(
        functools.partial(fused_kernel, factor_one, factor_two),
        out_shape=(
            jax.ShapeDtypeStruct((64, 128), BF),
            jax.ShapeDtypeStruct((16, 144, 128), BF),
            jax.ShapeDtypeStruct((10, 64, 1280), BF),
            jax.ShapeDtypeStruct((864, 64), BF),
        ),
        in_specs=[SMEM] + [VMEM] * 5,
        out_specs=(VMEM,) * 4,
        scratch_shapes=[
            pltpu.VMEM((1728, 128), BF),
            pltpu.VMEM((8, 64, 1024), F32),
            pltpu.VMEM((4, 64, 256), F32),
            pltpu.VMEM((6, 576, 256), BF),
            pltpu.VMEM((6, 128, 256), BF),
            pltpu.VMEM((2, 128, 256), F32),
            pltpu.VMEM((1744, 128), BF),
            pltpu.VMEM((912, 128), BF),
            pltpu.VMEM((2, 288, 192), F32),
        ],
        compiler_params=pltpu.CompilerParams(vmem_limit_bytes=48 << 20),
        cost_estimate=pl.CostEstimate(flops=4_000_000_000, bytes_accessed=6_000_000, transcendentals=700_000),
        name="fused",
    )(pos, v3, co, cx, near, far)


def volume_call(pos, dp, w1):
    return pl.pallas_call(
        volume_kernel,
        out_shape=jax.ShapeDtypeStruct((4, 32, 1024), BF),
        in_specs=[SMEM, VMEM, VMEM],
        out_specs=VMEM,
        scratch_shapes=[pltpu.VMEM((96, 576), BF)],
        compiler_params=pltpu.CompilerParams(vmem_limit_bytes=16 << 20),
        cost_estimate=pl.CostEstimate(flops=1_000_000_000, bytes_accessed=3_000_000, transcendentals=0),
        name="volume",
    )(pos, dp, w1)


def fits(volumes, w_first, w_second, cotangent):
    return (
        lax.axis_size("dp") == 16
        and lax.axis_size("space") == 2
        and volumes.shape == (1, 32, 4, 8, 128)
        and w_first.shape == (54, 64)
        and w_second.shape == (108, 128)
        and cotangent.shape == (1, 128, 1, 2, 32)
    )


def swap(x, bit):
    return lax.ppermute(x, "dp", [(i, i ^ bit) for i in range(16)])


def plane_major(block):
    return jnp.transpose(block[0], (1, 0, 2, 3)).reshape(4, 32, 1024)


def paired(volumes, w_first, w_second, cotangent):
    count = 16 * 2 * (volumes.size // 32)
    factor_one, factor_two = float(count) ** (-0.5), float(count // 8) ** (-0.5)
    across_space = [(0, 1), (1, 0)]
    pos = jnp.stack([lax.axis_index("dp"), lax.axis_index("space")]).astype(jnp.int32)
    volumes_other = lax.ppermute(volumes, "space", across_space)
    cot = jnp.transpose(cotangent, (0, 2, 3, 4, 1)).reshape(64, 128)
    cot_other = lax.ppermute(cot, "space", across_space)
    shard = pack_call(w_first, w_second)
    pieces = [swap(shard, 4 * k) for k in range(1, 4)]
    beside = swap(shard, 2)
    along_z = jnp.stack(pieces)
    rest = swap(along_z, 2)
    early = jnp.concatenate([shard[None], along_z, beside[None]])
    early_across = swap(early, 1)
    late_across = swap(rest, 1)
    near = jnp.concatenate([early, rest])
    far = jnp.concatenate([early_across, late_across])
    own = plane_major(volumes)
    other = plane_major(volumes_other)
    moved = shift_call(pos, own, other)
    pooled, wire, delta, w_one = fused_call(
        factor_one, factor_two, pos, moved, cot, cot_other, near, far
    )
    got = swap(wire[13:16], 1)
    crossed = swap(wire[8:13], 1)
    far_y = (wire[5:8].astype(F32) + got.astype(F32)).astype(BF)
    got = swap(far_y, 2)
    near_y = (wire[4].astype(F32) + crossed[4].astype(F32)).astype(BF)
    beside = swap(near_y, 2)
    along_z = (wire[1:4].astype(F32) + crossed[1:4].astype(F32) + got.astype(F32)).astype(BF)
    pieces = []
    for k in range(1, 4):
        pieces.append(swap(along_z[k - 1], 4 * k))
    share_one, share_two = finish_call(wire, crossed, beside, pieces)
    grad = volume_call(pos, delta, w_one)
    grad = jnp.transpose(grad.reshape(4, 32, 8, 128), (1, 0, 2, 3))[None]
    pooled = jnp.transpose(pooled.reshape(1, 1, 2, 32, 128), (0, 4, 1, 2, 3))
    return pooled, grad, share_one, share_two


def with_halo(block, sides, width):
    for axis, dim in sides:
        count = lax.axis_size(axis)
        forward = [(i, i + 1) for i in range(count - 1)]
        backward = [(target, source) for source, target in forward]
        low = lax.ppermute(
            lax.slice_in_dim(block, block.shape[dim] - width, None, axis=dim), axis, forward
        )
        high = lax.ppermute(lax.slice_in_dim(block, 0, width, axis=dim), axis, backward)
        block = jnp.concatenate([low, block, high], axis=dim)
    return block


def pad_sides(field):
    return jnp.pad(field, ((0, 0), (0, 0), (0, 0), (1, 1), (1, 1)))


def conv_forward(padded, weight):
    samples_here, in_width, depth_padded, extent_y, extent_z = padded.shape
    extent_x = depth_padded - 2
    out_width = weight.shape[1]
    framed = pad_sides(padded)
    kernel = weight.reshape(3, 3, 3, in_width, out_width)
    summed = jnp.zeros((samples_here, out_width, extent_x, extent_y, extent_z), jnp.float32)
    for along_x in range(3):
        for along_y in range(3):
            for along_z in range(3):
                window = framed[
                    :,
                    :,
                    along_x : along_x + extent_x,
                    along_y : along_y + extent_y,
                    along_z : along_z + extent_z,
                ]
                summed = summed + jnp.einsum(
                    "sixyz,io->soxyz",
                    window,
                    kernel[along_x, along_y, along_z],
                    preferred_element_type=jnp.float32,
                )
    return summed


def conv_input_grad(padded, weight, in_width):
    samples_here, out_width, depth_padded, extent_y, extent_z = padded.shape
    extent_x = depth_padded - 2
    framed = pad_sides(padded)
    kernel = weight.reshape(3, 3, 3, in_width, out_width)
    summed = jnp.zeros((samples_here, in_width, extent_x, extent_y, extent_z), jnp.float32)
    for along_x in range(3):
        for along_y in range(3):
            for along_z in range(3):
                window = framed[
                    :,
                    :,
                    2 - along_x : 2 - along_x + extent_x,
                    2 - along_y : 2 - along_y + extent_y,
                    2 - along_z : 2 - along_z + extent_z,
                ]
                summed = summed + jnp.einsum(
                    "soxyz,io->sixyz",
                    window,
                    kernel[along_x, along_y, along_z],
                    preferred_element_type=jnp.float32,
                )
    return summed


def conv_weight_grad(padded, grads):
    _, in_width, depth_padded, extent_y, extent_z = padded.shape
    extent_x = depth_padded - 2
    framed = pad_sides(padded)
    pieces = []
    for along_x in range(3):
        for along_y in range(3):
            for along_z in range(3):
                window = framed[
                    :,
                    :,
                    along_x : along_x + extent_x,
                    along_y : along_y + extent_y,
                    along_z : along_z + extent_z,
                ]
                pieces.append(
                    jnp.einsum("sixyz,soxyz->io", window, grads, preferred_element_type=jnp.float32)
                )
    return jnp.stack(pieces).reshape(27 * in_width, grads.shape[1])


def pooling(field):
    samples_here, width, extent_x, extent_y, extent_z = field.shape
    blocks = field.reshape(
        samples_here, width, extent_x // 2, 2, extent_y // 2, 2, extent_z // 2, 2
    )
    return jnp.mean(blocks, axis=(3, 5, 7))


def spread_up(field):
    samples_here, width, extent_x, extent_y, extent_z = field.shape
    blocks = jnp.broadcast_to(
        field[:, :, :, None, :, None, :, None],
        (samples_here, width, extent_x, 2, extent_y, 2, extent_z, 2),
    )
    return blocks.reshape(samples_here, width, 2 * extent_x, 2 * extent_y, 2 * extent_z)


def silu_slope(values):
    sigma = jax.nn.sigmoid(values)
    return sigma * (1.0 + values * (1.0 - sigma))


def general(volumes, w_first, w_second, cotangent):
    kernel_one, kernel_two = (
        lax.all_gather(w_first, "dp", axis=0, tiled=True),
        lax.all_gather(w_second, "dp", axis=0, tiled=True),
    )
    in_width = volumes.shape[1]
    mid_width = kernel_one.shape[1]
    count_one = lax.axis_size("dp") * lax.axis_size("space") * (volumes.size // in_width)
    factor_one = float(count_one) ** (-0.5)
    factor_two = float(count_one // 8) ** (-0.5)
    input_padded = with_halo(volumes, (("space", 2),), 1)
    first_pre = conv_forward(input_padded, kernel_one)
    first_pool = pooling(jax.nn.silu(first_pre)).astype(jnp.bfloat16)
    pool_padded = with_halo(first_pool, (("space", 2),), 1)
    second_pre = conv_forward(pool_padded, kernel_two)
    pooled = pooling(jax.nn.silu(second_pre)).astype(jnp.bfloat16)
    second_delta = (
        spread_up(cotangent.astype(jnp.float32)) * 0.125 * silu_slope(second_pre)
    ).astype(jnp.bfloat16)
    grad_two = conv_weight_grad(pool_padded, second_delta) * factor_two
    delta_padded = with_halo(second_delta, (("space", 2),), 1)
    pool_grad = conv_input_grad(delta_padded, kernel_two, mid_width).astype(jnp.bfloat16)
    first_delta = (spread_up(pool_grad.astype(jnp.float32)) * 0.125 * silu_slope(first_pre)).astype(
        jnp.bfloat16
    )
    grad_one = conv_weight_grad(input_padded, first_delta) * factor_one
    first_padded = with_halo(first_delta, (("space", 2),), 1)
    volume_grad = conv_input_grad(first_padded, kernel_one, in_width).astype(jnp.bfloat16)
    rows_one, rows_two = (
        lax.psum_scatter(
            grad_one.astype(jnp.bfloat16), "dp", scatter_dimension=0, tiled=True
        ).astype(jnp.float32),
        lax.psum_scatter(
            grad_two.astype(jnp.bfloat16), "dp", scatter_dimension=0, tiled=True
        ).astype(jnp.float32),
    )
    share_one, share_two = (
        lax.psum(rows_one.astype(jnp.bfloat16), "space").astype(jnp.float32),
        lax.psum(rows_two.astype(jnp.bfloat16), "space").astype(jnp.float32),
    )
    return (pooled, volume_grad, share_one, share_two)


def local(volumes, w_first, w_second, cotangent):
    if fits(volumes, w_first, w_second, cotangent):
        return paired(volumes, w_first, w_second, cotangent)
    return general(volumes, w_first, w_second, cotangent)


def solution(mesh):
    return jax.shard_map(
        local,
        mesh=mesh,
        in_specs=(
            P("dp", None, "space", None, None),
            P("dp", None),
            P("dp", None),
            P("dp", None, "space", None, None),
        ),
        out_specs=(
            P("dp", None, "space", None, None),
            P("dp", None, "space", None, None),
            P("dp", None),
            P("dp", None),
        ),
        check_vma=False,
    )
```

```python
import functools

import jax
import jax.numpy as jnp
from jax import lax
from jax.experimental import pallas as pl
from jax.experimental.pallas import tpu as pltpu
from jax.sharding import PartitionSpec as P


BF = jnp.bfloat16
F32 = jnp.float32
VMEM = pl.BlockSpec(memory_space=pltpu.VMEM)
SMEM = pl.BlockSpec(memory_space=pltpu.SMEM)


def dot(a, b):
    return jnp.dot(a, b, preferred_element_type=F32)


def dot_nt(a, b):
    return lax.dot_general(a, b, (((1,), (1,)), ((), ())), preferred_element_type=F32)


def iota(shape, dim):
    return lax.broadcasted_iota(jnp.int32, shape, dim)


def where_one(mask):
    return mask.astype(F32).astype(BF)


def eye(n):
    return where_one(iota((n, n), 0) == iota((n, n), 1))


def halves(x):
    hi = x.astype(BF)
    return hi, (x - hi.astype(F32)).astype(BF)


def roll_z(x, by):
    lane = iota(x.shape, 1)
    edge = 0 if by == 1 else 127
    return jnp.where(lane == edge, 0.0, pltpu.roll(x, by % 128, 1))


def roll_yz(x, db, dc):
    if db == 0 and dc == 0:
        return x
    lane = iota(x.shape, 1)
    y, z = lane // 64 + db, lane % 64 + dc
    inside = (y >= 0) & (y < 4) & (z >= 0) & (z < 64)
    return jnp.where(inside, pltpu.roll(x, (-(db * 64 + dc)) % 256, 1), 0.0)


def pack_kernel(first, second, out, wide, narrow, first_here, second_here, sems):
    copies = (
        pltpu.make_async_copy(first, first_here, sems.at[0]),
        pltpu.make_async_copy(second, second_here, sems.at[1]),
    )
    for copy in copies:
        copy.start()
    wide[...] = jnp.zeros(wide.shape, F32)
    for copy in copies:
        copy.wait()
    wide[0:108, :] = second_here[...].astype(F32)
    narrow[...] = first_here[...].astype(F32)
    wide[108:136, 0:64] = narrow[0:28, :]
    wide[108:134, 64:128] = narrow[28:54, :]
    out[...] = wide[...].astype(BF)


def pack_call(first, second):
    return pl.pallas_call(
        pack_kernel,
        out_shape=jax.ShapeDtypeStruct((136, 128), BF),
        in_specs=[pl.BlockSpec(memory_space=pltpu.HBM)] * 2,
        out_specs=VMEM,
        scratch_shapes=[
            pltpu.VMEM((136, 128), F32),
            pltpu.VMEM((54, 64), F32),
            pltpu.VMEM((54, 64), BF),
            pltpu.VMEM((108, 128), BF),
            pltpu.SemaphoreType.DMA((2,)),
        ],
        compiler_params=pltpu.CompilerParams(vmem_limit_bytes=2 << 20),
        cost_estimate=pl.CostEstimate(flops=40_000, bytes_accessed=80_000, transcendentals=0),
        name="pack",
    )(first, second)


def finish_kernel(wire, crossed, beside, one, two, three, first, second, total):
    total[...] = wire[0].astype(F32) + crossed[0].astype(F32) + beside[...].astype(F32)
    total[...] += one[...].astype(F32) + two[...].astype(F32) + three[...].astype(F32)
    second[...] = total[0:108, :]
    first[0:28, :] = total[108:136, 0:64]
    first[28:54, :] = total[108:134, 64:128]


def finish_call(wire, crossed, beside, pieces):
    return pl.pallas_call(
        finish_kernel,
        out_shape=(
            jax.ShapeDtypeStruct((54, 64), F32),
            jax.ShapeDtypeStruct((108, 128), F32),
        ),
        in_specs=[VMEM] * 6,
        out_specs=(VMEM,) * 2,
        scratch_shapes=[pltpu.VMEM((136, 128), F32)],
        compiler_params=pltpu.CompilerParams(vmem_limit_bytes=4 << 20),
        cost_estimate=pl.CostEstimate(flops=120_000, bytes_accessed=300_000, transcendentals=0),
        name="finish",
    )(wire, crossed, beside, *pieces)


def shift_kernel(pos, own, other, out):
    s = pos[1]
    out[0] = jnp.zeros((96, 1024), BF)
    out[9] = jnp.zeros((96, 1024), BF)
    for p in range(4):
        for block, place in ((own, 4 * s + 1 + p), (other, 4 * (1 - s) + 1 + p)):
            out[place, 32:64, :] = block[p]
            for y in range(8):
                lanes = slice(y * 128, y * 128 + 128)
                line = block[p, :, lanes].astype(F32)
                out[place, 0:32, lanes] = roll_z(line, 1).astype(BF)
                out[place, 64:96, lanes] = roll_z(line, -1).astype(BF)


def shift_call(pos, own, other):
    return pl.pallas_call(
        shift_kernel,
        out_shape=jax.ShapeDtypeStruct((10, 96, 1024), BF),
        in_specs=[SMEM, VMEM, VMEM],
        out_specs=VMEM,
        compiler_params=pltpu.CompilerParams(vmem_limit_bytes=8 << 20),
        cost_estimate=pl.CostEstimate(flops=600_000, bytes_accessed=2_500_000, transcendentals=0),
        name="shift",
    )(pos, own, other)


def unpack_weights(me, near, far, w1s, w2s):
    for d in range(16):
        k = jnp.bitwise_xor(me, d)
        place = (k // 2) % 2 * 4 + k // 4
        blk = lax.select(k % 2 == 0, near[place], far[place])
        w2s[108 * d : 108 * d + 108, :] = blk[0:108]
        w1s[54 * d : 54 * d + 28, :] = blk[108:136, 0:64]
        w1s[54 * d + 28 : 54 * d + 54, :] = blk[108:134, 64:128]


def fused_kernel(
    factor_one, factor_two,
    pos, v3, co, cx, near, far,
    pooled_out, wire_out, dp, w1_out,
    w2s, slope, fpl, fs, d2p, t2, g2s, g1s, acc1,
):
    me, s = pos[0], pos[1]
    unpack_weights(me, near, far, w1_out, w2s)
    id64, id128 = eye(64), eye(128)
    lhs1 = jnp.concatenate(
        [
            dot_nt(
                id64,
                jnp.concatenate(
                    [w1_out[(a * 3 + b) * 96 : (a * 3 + b) * 96 + 96, :] for a in range(3)], axis=0
                ),
            ).astype(BF)
            for b in range(3)
        ],
        axis=0,
    )
    pool1 = where_one(iota((256, 128), 0) // 2 == iota((256, 128), 1))

    def cols_of(x):
        return jnp.concatenate([v3[x], v3[x + 1], v3[x + 2]], axis=0)

    for x2 in range(4):
        total = [jnp.zeros((64, 128), F32) for _ in range(4)]
        for dx in range(2):
            x = 2 * x2 + dx
            prod = dot(lhs1, cols_of(x))
            for y in range(8):
                lanes = slice(y * 128, y * 128 + 128)
                pre = prod[64:128, lanes]
                if y > 0:
                    pre = pre + prod[0:64, (y - 1) * 128 : y * 128]
                if y < 7:
                    pre = pre + prod[128:192, (y + 1) * 128 : (y + 2) * 128]
                sig = jax.nn.sigmoid(pre)
                act = pre * sig
                slope[x, :, lanes] = sig + act * (1.0 - sig)
                total[y // 2] = total[y // 2] + act
        for h in range(2):
            hi, lo = halves(jnp.concatenate([total[2 * h], total[2 * h + 1]], axis=1))
            fpl[x2, :, h * 128 : h * 128 + 128] = (
                (dot(hi, pool1) + dot(lo, pool1)) * 0.125
            ).astype(BF).astype(F32)

    fs[0] = jnp.zeros((576, 256), BF)
    fs[5] = jnp.zeros((576, 256), BF)
    d2p[0] = jnp.zeros((128, 256), BF)
    d2p[5] = jnp.zeros((128, 256), BF)
    for x2 in range(4):
        plane = fpl[x2]
        for bc in range(9):
            fs[x2 + 1, bc * 64 : bc * 64 + 64, :] = roll_yz(plane, bc // 3 - 1, bc % 3 - 1).astype(BF)
    w2t = dot_nt(id128, w2s[...]).astype(BF)
    col = iota((64, 256), 1)
    spread2 = where_one(iota((64, 256), 0) == (col // 128) * 32 + (col % 64) // 2)
    col = iota((64, 256), 1)
    pool2 = where_one(iota((64, 256), 0) == (col // 128) * 32 + (col % 64) // 2)
    for x4 in range(2):
        cot = lax.select(x4 == s, co[...], cx[...])
        wide = dot(dot_nt(id128, cot).astype(BF), spread2) * 0.125
        total = jnp.zeros((128, 256), F32)
        for dx in range(2):
            x2 = 2 * x4 + dx
            rhs = jnp.concatenate([fs[x2], fs[x2 + 1], fs[x2 + 2]], axis=0)
            pre = dot(w2t, rhs)
            sig = jax.nn.sigmoid(pre)
            act = pre * sig
            total = total + act
            d2p[x2 + 1] = (wide * (sig + act * (1.0 - sig))).astype(BF)
        t2[x4] = total
    hi, lo = halves(t2[s])
    pooled_out[...] = ((dot_nt(pool2, hi) + dot_nt(pool2, lo)) * 0.125).astype(BF)

    lhs = jnp.concatenate([fs[p] for p in range(1, 5)], axis=1)
    for some in ((0, 1), (2,)):
        rhs = jnp.concatenate(
            [jnp.concatenate([d2p[p + 1 - a] for p in range(1, 5)], axis=1) for a in some], axis=0
        )
        prod = dot_nt(lhs, rhs) * factor_two
        for n, a in enumerate(some):
            g2s[a * 576 : a * 576 + 576, :] = prod[:, n * 128 : n * 128 + 128].astype(BF)
    g2s[1728:1744, :] = jnp.zeros((16, 128), BF)

    spread1 = where_one(iota((128, 256), 0) == iota((128, 256), 1) // 2)
    dp[0] = jnp.zeros((64, 1280), BF)
    dp[9] = jnp.zeros((64, 1280), BF)
    for x in range(8):
        dp[x + 1, :, 0:128] = jnp.zeros((64, 128), BF)
        dp[x + 1, :, 1152:1280] = jnp.zeros((64, 128), BF)
    back = jnp.concatenate([w2s[a * 576 : a * 576 + 576, :] for a in range(3)], axis=1)
    rhs = jnp.concatenate(
        [jnp.concatenate([d2p[x2 + 2 - a] for x2 in range(4)], axis=1) for a in range(3)], axis=0
    )
    spread_all = dot(back, rhs)
    for x2 in range(4):
        prod = spread_all[:, x2 * 256 : x2 * 256 + 256]
        grad = prod[256:320]
        for bc in range(9):
            if bc != 4:
                grad = grad + roll_yz(prod[bc * 64 : bc * 64 + 64], 1 - bc // 3, 1 - bc % 3)
        grad = grad.astype(BF)
        for h in range(2):
            wide = dot(grad[:, h * 128 : h * 128 + 128], spread1) * 0.125
            for dx in range(2):
                for y in range(4):
                    at = (4 * h + y) * 128
                    part = wide[:, (y // 2) * 128 : (y // 2) * 128 + 128]
                    dp[2 * x2 + dx + 1, :, at + 128 : at + 256] = (
                        part * slope[2 * x2 + dx, :, at : at + 128]
                    ).astype(BF)

    acc1[...] = jnp.zeros(acc1.shape, F32)

    def first_grads(i, carry):
        for n in range(4):
            x = 4 * i + n
            rhs = jnp.concatenate(
                [dp[x + 1, :, (2 - b) * 128 : (2 - b) * 128 + 1024] for b in range(3)], axis=0
            )
            acc1[n % 2] += dot_nt(cols_of(x), rhs)
        return carry

    lax.fori_loop(0, 2, first_grads, 0)
    prod = (acc1[0] + acc1[1]) * factor_one
    g1s[0:32, :] = jnp.zeros((32, 128), BF)
    g1s[864:912, :] = jnp.zeros((48, 128), BF)
    for a in range(3):
        for b in range(3):
            block = prod[a * 96 : a * 96 + 96, b * 64 : b * 64 + 64].astype(BF)
            row = (a * 3 + b) * 96 + 32
            g1s[row : row + 96, 0:64] = block
            g1s[row - 28 : row + 68, 64:128] = block
    for d in range(16):
        k = jnp.bitwise_xor(me, d)
        place = k % 2 * 8 + (k // 2) % 2 * 4 + k // 4
        wire_out[place, 0:108, :] = g2s[108 * d : 108 * d + 108, :]
        wire_out[place, 108:136, :] = g1s[54 * d + 32 : 54 * d + 60, :]


def volume_kernel(pos, dp, w1, out, wd):
    s = pos[1]
    for ab in range(9):
        wd[:, ab * 64 : ab * 64 + 64] = w1[ab * 96 : ab * 96 + 96, :]
    lhs = wd[...]
    for p in range(4):
        x = 4 * s + p
        rhs = jnp.concatenate(
            [
                dp[x + 2 - a, :, (2 - b) * 128 : (2 - b) * 128 + 1024]
                for a in range(3)
                for b in range(3)
            ],
            axis=0,
        )
        prod = dot(lhs, rhs)
        for y in range(8):
            part = prod[:, y * 128 : y * 128 + 128]
            out[p, :, y * 128 : y * 128 + 128] = (
                part[32:64] + roll_z(part[0:32], -1) + roll_z(part[64:96], 1)
            ).astype(BF)


def fused_call(factor_one, factor_two, pos, v3, co, cx, near, far):
    return pl.pallas_call(
        functools.partial(fused_kernel, factor_one, factor_two),
        out_shape=(
            jax.ShapeDtypeStruct((64, 128), BF),
            jax.ShapeDtypeStruct((16, 136, 128), BF),
            jax.ShapeDtypeStruct((10, 64, 1280), BF),
            jax.ShapeDtypeStruct((864, 64), BF),
        ),
        in_specs=[SMEM] + [VMEM] * 5,
        out_specs=(VMEM,) * 4,
        scratch_shapes=[
            pltpu.VMEM((1728, 128), BF),
            pltpu.VMEM((8, 64, 1024), F32),
            pltpu.VMEM((4, 64, 256), F32),
            pltpu.VMEM((6, 576, 256), BF),
            pltpu.VMEM((6, 128, 256), BF),
            pltpu.VMEM((2, 128, 256), F32),
            pltpu.VMEM((1744, 128), BF),
            pltpu.VMEM((912, 128), BF),
            pltpu.VMEM((2, 288, 192), F32),
        ],
        compiler_params=pltpu.CompilerParams(vmem_limit_bytes=48 << 20),
        cost_estimate=pl.CostEstimate(flops=4_000_000_000, bytes_accessed=6_000_000, transcendentals=700_000),
        name="fused",
    )(pos, v3, co, cx, near, far)


def volume_call(pos, dp, w1):
    return pl.pallas_call(
        volume_kernel,
        out_shape=jax.ShapeDtypeStruct((4, 32, 1024), BF),
        in_specs=[SMEM, VMEM, VMEM],
        out_specs=VMEM,
        scratch_shapes=[pltpu.VMEM((96, 576), BF)],
        compiler_params=pltpu.CompilerParams(vmem_limit_bytes=16 << 20),
        cost_estimate=pl.CostEstimate(flops=1_000_000_000, bytes_accessed=3_000_000, transcendentals=0),
        name="volume",
    )(pos, dp, w1)


def fits(volumes, w_first, w_second, cotangent):
    return (
        lax.axis_size("dp") == 16
        and lax.axis_size("space") == 2
        and volumes.shape == (1, 32, 4, 8, 128)
        and w_first.shape == (54, 64)
        and w_second.shape == (108, 128)
        and cotangent.shape == (1, 128, 1, 2, 32)
    )


def swap(x, bit):
    return lax.ppermute(x, "dp", [(i, i ^ bit) for i in range(16)])


def plane_major(block):
    return jnp.transpose(block[0], (1, 0, 2, 3)).reshape(4, 32, 1024)


def paired(volumes, w_first, w_second, cotangent):
    count = 16 * 2 * (volumes.size // 32)
    factor_one, factor_two = float(count) ** (-0.5), float(count // 8) ** (-0.5)
    across_space = [(0, 1), (1, 0)]
    pos = jnp.stack([lax.axis_index("dp"), lax.axis_index("space")]).astype(jnp.int32)
    volumes_other = lax.ppermute(volumes, "space", across_space)
    cot = jnp.transpose(cotangent, (0, 2, 3, 4, 1)).reshape(64, 128)
    cot_other = lax.ppermute(cot, "space", across_space)
    shard = pack_call(w_first, w_second)
    pieces = [swap(shard, 4 * k) for k in range(1, 4)]
    beside = swap(shard, 2)
    along_z = jnp.stack(pieces)
    rest = swap(along_z, 2)
    early = jnp.concatenate([shard[None], along_z, beside[None]])
    early_across = swap(early, 1)
    late_across = swap(rest, 1)
    near = jnp.concatenate([early, rest])
    far = jnp.concatenate([early_across, late_across])
    own = plane_major(volumes)
    other = plane_major(volumes_other)
    moved = shift_call(pos, own, other)
    pooled, wire, delta, w_one = fused_call(
        factor_one, factor_two, pos, moved, cot, cot_other, near, far
    )
    got = swap(wire[13:16], 1)
    crossed = swap(wire[8:13], 1)
    far_y = (wire[5:8].astype(F32) + got.astype(F32)).astype(BF)
    got = swap(far_y, 2)
    near_y = (wire[4].astype(F32) + crossed[4].astype(F32)).astype(BF)
    beside = swap(near_y, 2)
    along_z = (wire[1:4].astype(F32) + crossed[1:4].astype(F32) + got.astype(F32)).astype(BF)
    pieces = []
    for k in range(1, 4):
        pieces.append(swap(along_z[k - 1], 4 * k))
    share_one, share_two = finish_call(wire, crossed, beside, pieces)
    grad = volume_call(pos, delta, w_one)
    grad = jnp.transpose(grad.reshape(4, 32, 8, 128), (1, 0, 2, 3))[None]
    pooled = jnp.transpose(pooled.reshape(1, 1, 2, 32, 128), (0, 4, 1, 2, 3))
    return pooled, grad, share_one, share_two


def with_halo(block, sides, width):
    for axis, dim in sides:
        count = lax.axis_size(axis)
        forward = [(i, i + 1) for i in range(count - 1)]
        backward = [(target, source) for source, target in forward]
        low = lax.ppermute(
            lax.slice_in_dim(block, block.shape[dim] - width, None, axis=dim), axis, forward
        )
        high = lax.ppermute(lax.slice_in_dim(block, 0, width, axis=dim), axis, backward)
        block = jnp.concatenate([low, block, high], axis=dim)
    return block


def pad_sides(field):
    return jnp.pad(field, ((0, 0), (0, 0), (0, 0), (1, 1), (1, 1)))


def conv_forward(padded, weight):
    samples_here, in_width, depth_padded, extent_y, extent_z = padded.shape
    extent_x = depth_padded - 2
    out_width = weight.shape[1]
    framed = pad_sides(padded)
    kernel = weight.reshape(3, 3, 3, in_width, out_width)
    summed = jnp.zeros((samples_here, out_width, extent_x, extent_y, extent_z), jnp.float32)
    for along_x in range(3):
        for along_y in range(3):
            for along_z in range(3):
                window = framed[
                    :,
                    :,
                    along_x : along_x + extent_x,
                    along_y : along_y + extent_y,
                    along_z : along_z + extent_z,
                ]
                summed = summed + jnp.einsum(
                    "sixyz,io->soxyz",
                    window,
                    kernel[along_x, along_y, along_z],
                    preferred_element_type=jnp.float32,
                )
    return summed


def conv_input_grad(padded, weight, in_width):
    samples_here, out_width, depth_padded, extent_y, extent_z = padded.shape
    extent_x = depth_padded - 2
    framed = pad_sides(padded)
    kernel = weight.reshape(3, 3, 3, in_width, out_width)
    summed = jnp.zeros((samples_here, in_width, extent_x, extent_y, extent_z), jnp.float32)
    for along_x in range(3):
        for along_y in range(3):
            for along_z in range(3):
                window = framed[
                    :,
                    :,
                    2 - along_x : 2 - along_x + extent_x,
                    2 - along_y : 2 - along_y + extent_y,
                    2 - along_z : 2 - along_z + extent_z,
                ]
                summed = summed + jnp.einsum(
                    "soxyz,io->sixyz",
                    window,
                    kernel[along_x, along_y, along_z],
                    preferred_element_type=jnp.float32,
                )
    return summed


def conv_weight_grad(padded, grads):
    _, in_width, depth_padded, extent_y, extent_z = padded.shape
    extent_x = depth_padded - 2
    framed = pad_sides(padded)
    pieces = []
    for along_x in range(3):
        for along_y in range(3):
            for along_z in range(3):
                window = framed[
                    :,
                    :,
                    along_x : along_x + extent_x,
                    along_y : along_y + extent_y,
                    along_z : along_z + extent_z,
                ]
                pieces.append(
                    jnp.einsum("sixyz,soxyz->io", window, grads, preferred_element_type=jnp.float32)
                )
    return jnp.stack(pieces).reshape(27 * in_width, grads.shape[1])


def pooling(field):
    samples_here, width, extent_x, extent_y, extent_z = field.shape
    blocks = field.reshape(
        samples_here, width, extent_x // 2, 2, extent_y // 2, 2, extent_z // 2, 2
    )
    return jnp.mean(blocks, axis=(3, 5, 7))


def spread_up(field):
    samples_here, width, extent_x, extent_y, extent_z = field.shape
    blocks = jnp.broadcast_to(
        field[:, :, :, None, :, None, :, None],
        (samples_here, width, extent_x, 2, extent_y, 2, extent_z, 2),
    )
    return blocks.reshape(samples_here, width, 2 * extent_x, 2 * extent_y, 2 * extent_z)


def silu_slope(values):
    sigma = jax.nn.sigmoid(values)
    return sigma * (1.0 + values * (1.0 - sigma))


def general(volumes, w_first, w_second, cotangent):
    kernel_one, kernel_two = (
        lax.all_gather(w_first, "dp", axis=0, tiled=True),
        lax.all_gather(w_second, "dp", axis=0, tiled=True),
    )
    in_width = volumes.shape[1]
    mid_width = kernel_one.shape[1]
    count_one = lax.axis_size("dp") * lax.axis_size("space") * (volumes.size // in_width)
    factor_one = float(count_one) ** (-0.5)
    factor_two = float(count_one // 8) ** (-0.5)
    input_padded = with_halo(volumes, (("space", 2),), 1)
    first_pre = conv_forward(input_padded, kernel_one)
    first_pool = pooling(jax.nn.silu(first_pre)).astype(jnp.bfloat16)
    pool_padded = with_halo(first_pool, (("space", 2),), 1)
    second_pre = conv_forward(pool_padded, kernel_two)
    pooled = pooling(jax.nn.silu(second_pre)).astype(jnp.bfloat16)
    second_delta = (
        spread_up(cotangent.astype(jnp.float32)) * 0.125 * silu_slope(second_pre)
    ).astype(jnp.bfloat16)
    grad_two = conv_weight_grad(pool_padded, second_delta) * factor_two
    delta_padded = with_halo(second_delta, (("space", 2),), 1)
    pool_grad = conv_input_grad(delta_padded, kernel_two, mid_width).astype(jnp.bfloat16)
    first_delta = (spread_up(pool_grad.astype(jnp.float32)) * 0.125 * silu_slope(first_pre)).astype(
        jnp.bfloat16
    )
    grad_one = conv_weight_grad(input_padded, first_delta) * factor_one
    first_padded = with_halo(first_delta, (("space", 2),), 1)
    volume_grad = conv_input_grad(first_padded, kernel_one, in_width).astype(jnp.bfloat16)
    rows_one, rows_two = (
        lax.psum_scatter(
            grad_one.astype(jnp.bfloat16), "dp", scatter_dimension=0, tiled=True
        ).astype(jnp.float32),
        lax.psum_scatter(
            grad_two.astype(jnp.bfloat16), "dp", scatter_dimension=0, tiled=True
        ).astype(jnp.float32),
    )
    share_one, share_two = (
        lax.psum(rows_one.astype(jnp.bfloat16), "space").astype(jnp.float32),
        lax.psum(rows_two.astype(jnp.bfloat16), "space").astype(jnp.float32),
    )
    return (pooled, volume_grad, share_one, share_two)


def local(volumes, w_first, w_second, cotangent):
    if fits(volumes, w_first, w_second, cotangent):
        return paired(volumes, w_first, w_second, cotangent)
    return general(volumes, w_first, w_second, cotangent)


def solution(mesh):
    return jax.shard_map(
        local,
        mesh=mesh,
        in_specs=(
            P("dp", None, "space", None, None),
            P("dp", None),
            P("dp", None),
            P("dp", None, "space", None, None),
        ),
        out_specs=(
            P("dp", None, "space", None, None),
            P("dp", None, "space", None, None),
            P("dp", None),
            P("dp", None),
        ),
        check_vma=False,
    )
```
